256 devices in a mesh: sec: 16 (over y, x), own: 16 (over z, core).
Axes of the slice: x: 4, y: 4, z: 8, core: 2. Of those that a mesh axis runs over, the one named last changes fastest.
Arguments:
- right_sides: float32 [2, 128, 65536], P(None, None, ('sec', 'own')), may hold values from -6 to 6
- inv_diag: float32 [65536, 256], P(('sec', 'own')), may hold values from -1 to 2, as said below
- factor_tiles: bfloat16 [65536, 4096], P(('sec', 'own')), may hold values from -0.046875 to 0.046875
- structure: int32 [256, 16], P(('sec', 'own')), may hold values 0 or 1
- ancestor: int32 [16, 16], P('sec'), may hold values from 0 to 15, each once within a row
- carried: float32 [128, 65536], P(None, ('sec', 'own')), may hold values from -4 to 4
Outputs:
- solution: float32 [2, 128, 65536], P(None, None, ('sec', 'own'))
- carry_out: float32 [128, 65536], P(None, ('sec', 'own'))
The draws below stay inside these ranges and needn't reach their ends.
Inputs may be any that keep to these rules, and one draw needn't show every extreme that they name: `inv_diag`: each diagonal block is the identity plus a dense part of moderate size. `ancestor`: each row is a permutation of 0 to 15.
All inputs are finite; a program needn't handle non-finite values. No bound on the sum of `structure` on one device may be relied on, other than what follows from the above.
Results may differ from the reference program's by a relative error of at most 0.0003.
Values sent between devices are 32-bit elements; how exact they have to be, the bound alone decides.
No kernel may reach another device: no remote copies, remote signals or barrier semaphores. Data moves between devices by JAX's collectives and lax.ppermute only.
A program may use at most 64 MiB of HBM per device.

```python
import math
import jax
import jax.numpy as jnp
from jax import lax

B = 256
CHAIN = 128
TICKS = 2
SECTIONS = 16
OWNERS = 16
ANC = 16
ROWS = 65536


def draw_inv_diag(key, part):
    noise = jnp.clip(jax.random.normal(key, (ROWS, B), jnp.float32), -4.0, 4.0)
    factor = 0.5
    identity = jnp.tile(jnp.eye(B, dtype=jnp.float32), (ROWS // B, 1))
    return identity + factor * noise / math.sqrt(B)


def plant(array, own_key, least, largest):
    longest = array.shape.index(max(array.shape))
    spots = []
    for shift in (0, 1):
        where = [jax.random.randint(jax.random.fold_in(own_key, axis), (), 0, length) for axis, length in enumerate(array.shape)]
        where[longest] = (where[longest] + shift) % array.shape[longest]
        spots.append(tuple(where))
    return array.at[spots[0]].set(least).at[spots[1]].set(largest)


def block_scale(stream_key, shape, split, least, largest):
    def one(dim, blocks):
        draws = jax.random.uniform(jax.random.fold_in(jax.random.fold_in(stream_key, 6), dim), (blocks,), jnp.float32, least / len(split), largest / len(split))
        return jnp.repeat(jnp.exp(draws), shape[dim] // blocks).reshape((-1,) + (1,) * (len(shape) - dim - 1))

    factor_of = one(*split[0])
    for cut in split[1:]:
        factor_of = factor_of * one(*cut)
    return factor_of


def bell_draw(key, dims, width, reach, cuts=(), held_as=jnp.bfloat16):
    entries = jax.random.normal(key, dims, jnp.float32) * width
    if len(cuts) > 0:
        entries = block_scale(key, dims, cuts, -0.22, 0.18) * entries
    return jnp.clip(entries, min=-reach, max=reach).astype(held_as)


def setup_inputs(seed: int = 0) -> dict:
    keys = jax.random.split(jax.random.key(seed), 7)
    right_sides = bell_draw(keys[0], (TICKS, CHAIN, ROWS), 1.0, 6.0, ((2, 256),), jnp.float32)
    inv_diag = draw_inv_diag(jax.random.fold_in(keys[6], 71), 0)
    factor_tiles = bell_draw(keys[2], (ROWS, ANC * B), (4 * B * OWNERS) ** -0.5, 0.046875, ((0, 256),))
    structure = plant((jax.random.randint(keys[3], (SECTIONS * OWNERS, ANC), 0, 4) < 3).astype(jnp.int32), jax.random.fold_in(keys[3], 1), 0, 1)
    ancestor = jax.vmap(lambda own: jax.random.permutation(own, ANC))(jax.random.split(keys[4], SECTIONS)).reshape((SECTIONS, ANC)).astype(jnp.int32)
    carried = bell_draw(keys[5], (CHAIN, ROWS), 0.5, 4.0, ((1, 256),), jnp.float32)
    return dict(right_sides=right_sides, inv_diag=inv_diag, factor_tiles=factor_tiles, structure=structure, ancestor=ancestor, carried=carried)


def reference(right_sides, inv_diag, factor_tiles, structure, ancestor, carried):
    blocks = SECTIONS * OWNERS
    highest = lax.Precision.HIGHEST
    inverse = inv_diag.reshape(blocks, B, B)
    factor = factor_tiles.astype(jnp.float32).reshape(blocks, B, ANC * B)
    slot_target = jnp.repeat(ancestor, OWNERS, axis=0)
    selector = structure.astype(jnp.float32)[:, :, None] * (slot_target[:, :, None] == jnp.arange(ANC, dtype=jnp.int32)[None, None, :]).astype(jnp.float32)
    incoming = carried.reshape(CHAIN, blocks, B)
    solved_all = []
    for tick_index in range(TICKS):
        residual = right_sides[tick_index].reshape(CHAIN, blocks, B) - incoming
        solved = jnp.einsum('cki,kij->ckj', residual, inverse, precision=highest)
        solved_all.append(solved.reshape(CHAIN, ROWS))
        partial_value = jnp.einsum('cki,kin->ckn', solved, factor, precision=highest).reshape(CHAIN, blocks, ANC, B)
        routed = jnp.einsum('ckab,kaj->ckjb', partial_value, selector, precision=highest)
        per_section = routed.reshape(CHAIN, SECTIONS, OWNERS, ANC, B).sum(axis=2)
        shifted = jnp.concatenate([jnp.zeros((CHAIN, 1, ANC, B), jnp.float32), per_section[:, :-1]], axis=1)
        incoming = shifted.reshape(CHAIN, blocks, B)
    return jnp.stack(solved_all), incoming.reshape(CHAIN, ROWS)
```

```python
import functools

import jax
import jax.numpy as jnp
from jax import lax
from jax.experimental import pallas as pl
from jax.experimental.pallas import tpu as pltpu
from jax.sharding import PartitionSpec as P

STREAMS = 2


def split(value):
    high = value.astype(jnp.bfloat16)
    return high, (value - high.astype(jnp.float32)).astype(jnp.bfloat16)


def dot(a, b):
    return jnp.dot(a, b, preferred_element_type=jnp.float32)


def local_kernel(
    chips,
    ancestor,
    structure,
    right_side,
    incoming,
    inverse,
    factor,
    solved,
    keep4,
    keep3,
    keep2,
    keep1,
    keep0,
    give_early,
    give_late,
    slot_of,
):
    rows, block = right_side.shape
    slots = ancestor.shape[1]
    for slot in range(slots):
        slot_of[ancestor[0, slot]] = slot
    me = lax.axis_index("own")
    chip, core = me // 2, me % 2
    ahead = 1 - 2 * core

    inverse_high, inverse_low = split(inverse[...])
    high, low = split(right_side[...] - incoming[...])
    both = dot(jnp.concatenate([high, low], axis=0), inverse_high)
    result = both[:rows] + both[rows:] + dot(high, inverse_low)
    solved[...] = result
    lhs = jnp.concatenate(split(result), axis=0)

    def product(distance, to_core):
        target = ((chip + distance + chips) % chips) * 2 + to_core
        slot = slot_of[target]
        tile = factor[:, pl.ds(pl.multiple_of(slot * block, block), block)]
        both = dot(lhs, tile)
        return (both[:rows] + both[rows:]) * structure[0, slot].astype(jnp.float32)

    far = chips // 2
    keep4[...] = product(far, core)
    give_early[0] = product(far, 1 - core)
    for place, (ref, first, distance) in enumerate(
        ((give_early, 1, 3), (give_late, 0, 2), (give_late, 2, 1))
    ):
        ref[first] = product(-distance * ahead, 1 - core)
        ref[first + 1] = product(-distance * ahead, core)
    give_late[4] = product(0, 1 - core)
    for ref, distance in ((keep3, 3), (keep2, 2), (keep1, 1)):
        ref[0] = product(distance * ahead, core)
        ref[1] = product(distance * ahead, 1 - core)
    keep0[...] = product(0, core)


def local_step(chips, ancestor, structure, right_side, incoming, inverse, factor):
    rows, block = right_side.shape
    shapes = [(rows, block), (rows, block)] + [(2, rows, block)] * 3
    shapes += [(rows, block), (3, rows, block), (5, rows, block)]
    vmem = pl.BlockSpec(memory_space=pltpu.VMEM)
    smem = pl.BlockSpec(memory_space=pltpu.SMEM)
    return pl.pallas_call(
        functools.partial(local_kernel, chips),
        out_shape=[jax.ShapeDtypeStruct(shape, jnp.float32) for shape in shapes],
        in_specs=[smem, smem, vmem, vmem, vmem, vmem],
        out_specs=[vmem] * len(shapes),
        scratch_shapes=[pltpu.SMEM((ancestor.shape[1],), jnp.int32)],
        compiler_params=pltpu.CompilerParams(vmem_limit_bytes=12 << 20),
        cost_estimate=pl.CostEstimate(
            flops=2 * 2 * rows * block * block * 18,
            bytes_accessed=4 << 20,
            transcendentals=0,
        ),
    )(ancestor, structure, right_side, incoming, inverse, factor)


def shards(right_sides, inv_diag, factor_tiles, structure, ancestor, carried):
    owners = lax.axis_size("own")
    sections = lax.axis_size("sec")
    chips = owners // 2
    partner = [(i, i ^ 1) for i in range(owners)]
    ring = [
        (i, ((i // 2 + 1 - 2 * (i % 2)) % chips) * 2 + i % 2) for i in range(owners)
    ]
    onward = [(i, i + 1) for i in range(sections - 1)]
    ticks, chain, _ = right_sides.shape
    rows = chain // STREAMS

    swap = lambda value: lax.ppermute(value, "own", partner)
    pass_on = lambda value: lax.ppermute(value, "own", ring)

    incoming = [carried[i * rows : (i + 1) * rows] for i in range(STREAMS)]
    solved_all = []
    for tick in range(ticks):
        solved_here = []
        for stream in range(STREAMS):
            right_side = right_sides[tick, stream * rows : (stream + 1) * rows]
            solved, keep4, keep3, keep2, keep1, keep0, early, late = local_step(
                chips,
                ancestor,
                structure,
                right_side,
                incoming[stream],
                inv_diag,
                factor_tiles,
            )
            solved_here.append(solved)
            early = swap(early)
            late = swap(late)
            moving = pass_on(keep4 + early[0])
            moving = jnp.stack(
                [keep3[0] + early[1] + moving, keep3[1] + early[2]]
            )
            moving = pass_on(moving)
            moving = pass_on(keep2 + late[0:2] + moving)
            moving = pass_on(keep1 + late[2:4] + moving)
            crossed = swap(moving[1])
            total = moving[0] + (keep0 + late[4]) + crossed
            incoming[stream] = lax.ppermute(total, "sec", onward)
        solved_all.append(jnp.concatenate(solved_here, axis=0))
    return jnp.stack(solved_all), jnp.concatenate(incoming, axis=0)


def solution(mesh):
    in_specs = (
        P(None, None, ("sec", "own")),
        P(("sec", "own"), None),
        P(("sec", "own"), None),
        P(("sec", "own"), None),
        P("sec", None),
        P(None, ("sec", "own")),
    )
    out_specs = (P(None, None, ("sec", "own")), P(None, ("sec", "own")))
    return jax.shard_map(
        shards, mesh=mesh, in_specs=in_specs, out_specs=out_specs, check_vma=False
    )
```

```python
import functools

import jax
import jax.numpy as jnp
from jax import lax
from jax.experimental import pallas as pl
from jax.experimental.pallas import tpu as pltpu
from jax.sharding import PartitionSpec as P

STREAMS = 2


def split(value):
    high = value.astype(jnp.bfloat16)
    return high, (value - high.astype(jnp.float32)).astype(jnp.bfloat16)


def dot(a, b):
    return jnp.dot(a, b, preferred_element_type=jnp.float32)


def product(table, lhs, factor, place, distance, to_core):
    chips, chip = place
    rows, block = lhs.shape[0] // 2, lhs.shape[1]
    target = ((chip + distance + chips) % chips) * 2 + to_core
    start = pl.multiple_of(table[0, target] * block, block)
    both = dot(lhs, factor[:, pl.ds(start, block)])
    return (both[:rows] + both[rows:]) * table[1, target].astype(jnp.float32)


def position(chips):
    me = lax.axis_index("own")
    chip, core = me // 2, me % 2
    return (chips, chip), core, 1 - 2 * ((chip + core) % 2)


def solve(residual, inverse_high, inverse_low):
    rows = residual.shape[0]
    high, low = split(residual)
    both = dot(jnp.concatenate([high, low], axis=0), inverse_high)
    result = both[:rows] + both[rows:] + dot(high, inverse_low)
    return result, jnp.concatenate(split(result), axis=0)


def farthest(table, lhs, factor, chips, early, keep4):
    place, core, ahead = position(chips)
    rows = keep4[0].shape[0]
    mine = (core + 3) % 2
    for slot, distance, to_core in (
        (0, chips // 2, 1 - core),
        (None, chips // 2, core),
        (1, -3 * ahead, 1 - mine),
        (2, -3 * ahead, mine),
    ):
        value = product(table, lhs, factor, place, distance, to_core)
        for stream in range(len(keep4)):
            part = value[stream * rows : (stream + 1) * rows]
            if slot is None:
                keep4[stream][...] = part
            else:
                early[stream][slot] = part


def first_kernel(
    chips, streams, ancestor, structure, right_sides, carried, inverse, factor,
    table, factor_here, inverse_high, inverse_low, solved, lhs, *rest,
):
    early, keep4 = rest[:streams], rest[streams : 2 * streams]
    slots, present, right_here, carried_here, inverse_here, sems = rest[2 * streams :]
    copies = [
        pltpu.make_async_copy(source, target, sems.at[i])
        for i, (source, target) in enumerate(
            (
                (inverse, inverse_here),
                (right_sides.at[0], right_here),
                (carried, carried_here),
                (ancestor, slots),
                (structure, present),
                (factor, factor_here),
            )
        )
    ]
    for copy in copies:
        copy.start()
    for copy in copies[:3]:
        copy.wait()
    inverse_high[...], inverse_low[...] = split(inverse_here[...])
    solved[...], lhs[...] = solve(
        right_here[...] - carried_here[...], inverse_high[...], inverse_low[...]
    )
    copies[3].wait()
    copies[4].wait()
    for slot in range(slots.shape[1]):
        table[0, slots[0, slot]] = slot
        table[1, slots[0, slot]] = present[0, slot]
    copies[5].wait()
    farthest(table, lhs[...], factor_here, chips, early, keep4)


def next_kernel(
    chips, tick, first_row, table, right_sides, moving, own, crossed,
    inverse_high, inverse_low, factor, solved, lhs, early, keep4,
):
    here = pl.ds(first_row, solved.shape[0])
    incoming = moving[0] + own[here] + crossed[...]
    incoming = jnp.where(lax.axis_index("sec") == 0, 0.0, incoming)
    solved[...], lhs[...] = solve(
        right_sides[tick, here] - incoming, inverse_high[...], inverse_low[...]
    )
    farthest(table, lhs[...], factor, chips, [early], [keep4])


def late_kernel(chips, streams, table, lhs, factor, *outs):
    place, core, ahead = position(chips)
    value = lhs[...]
    rows = value.shape[0] // 2 // streams
    late, keep3, keep2, keep1, keep0 = (
        outs[i * streams : (i + 1) * streams] for i in range(5)
    )

    def put(refs, index, distance, to_core):
        whole = product(table, value, factor, place, distance, to_core)
        for stream, ref in enumerate(refs):
            ref[index] = whole[stream * rows : (stream + 1) * rows]

    for distance, give, keep in ((2, 0, keep2), (1, 2, keep1), (3, None, keep3)):
        mine = (core + distance) % 2
        if give is not None:
            put(late, give, -distance * ahead, 1 - mine)
            put(late, give + 1, -distance * ahead, mine)
        put(keep, 0, distance * ahead, mine)
        put(keep, 1, distance * ahead, 1 - mine)
    put(late, 4, 0, 1 - core)
    put(keep0, ..., 0, core)


VMEM = pl.BlockSpec(memory_space=pltpu.VMEM)
SMEM = pl.BlockSpec(memory_space=pltpu.SMEM)
HBM = pl.BlockSpec(memory_space=pltpu.HBM)
F32 = functools.partial(jax.ShapeDtypeStruct, dtype=jnp.float32)
BF16 = functools.partial(jax.ShapeDtypeStruct, dtype=jnp.bfloat16)


def call(kernel, products, in_specs, outs, limit, scratch=()):
    return pl.pallas_call(
        kernel,
        out_shape=outs,
        in_specs=in_specs,
        out_specs=[SMEM if out.dtype == jnp.int32 else VMEM for out in outs],
        scratch_shapes=list(scratch),
        compiler_params=pltpu.CompilerParams(vmem_limit_bytes=limit << 20),
        cost_estimate=pl.CostEstimate(
            flops=products * 2 * 256 * 256 * 256,
            bytes_accessed=products * 65536 * 2,
            transcendentals=0,
        ),
    )


def first_step(chips, streams, rows, arrays):
    ancestor, _, _, carried, _, factor = arrays
    slots = ancestor.shape[1]
    width, block = carried.shape
    square = (block, block)
    outs = [jax.ShapeDtypeStruct((2, slots), jnp.int32), BF16(factor.shape)]
    outs += [BF16(square)] * 2 + [F32((width, block)), BF16((2 * width, block))]
    outs += [F32((3, rows, block))] * streams + [F32((rows, block))] * streams
    scratch = [
        pltpu.SMEM((1, slots), jnp.int32),
        pltpu.SMEM((1, slots), jnp.int32),
        pltpu.VMEM((width, block), jnp.float32),
        pltpu.VMEM((width, block), jnp.float32),
        pltpu.VMEM(square, jnp.float32),
        pltpu.SemaphoreType.DMA((6,)),
    ]
    kernel = functools.partial(first_kernel, chips, streams)
    out = call(kernel, 6, [HBM] * 6, outs, 4, scratch)(
        *[pltpu.with_memory_space_constraint(array, pltpu.HBM) for array in arrays]
    )
    fixed, (solved, lhs) = out[:4], out[4:6]
    return fixed, solved, lhs, out[6 : 6 + streams], out[6 + streams :]


def next_step(chips, tick, first_row, fixed, right_sides, moving, own, crossed):
    table, factor, inverse_high, inverse_low = fixed
    rows, block = crossed.shape
    outs = [F32((rows, block)), BF16((2 * rows, block))]
    outs += [F32((3, rows, block)), F32((rows, block))]
    kernel = functools.partial(next_kernel, chips, tick, first_row)
    return call(kernel, 6, [SMEM] + [VMEM] * 7, outs, 4)(
        table, right_sides, moving, own, crossed, inverse_high, inverse_low, factor
    )


def late_step(chips, streams, fixed, lhs):
    rows, block = lhs.shape[0] // 2 // streams, lhs.shape[1]
    shapes = [(5, rows, block)] + [(2, rows, block)] * 3 + [(rows, block)]
    outs = [F32(shape) for shape in shapes for _ in range(streams)]
    kernel = functools.partial(late_kernel, chips, streams)
    out = call(kernel, 12, [SMEM, VMEM, VMEM], outs, 4)(fixed[0], lhs, fixed[1])
    return [out[stream::streams] for stream in range(streams)]


def shards(right_sides, inv_diag, factor_tiles, structure, ancestor, carried):
    owners = lax.axis_size("own")
    sections = lax.axis_size("sec")
    chips = owners // 2
    partner = [(i, i ^ 1) for i in range(owners)]

    def next_on_chain(i):
        chip, core = i // 2, i % 2
        ahead = 1 - 2 * ((chip + core) % 2)
        return ((chip + ahead) % chips) * 2 + 1 - core

    def to_next_section(place):
        return [
            (s * owners + i, (s + 1) % sections * owners + place(i))
            for s in range(sections)
            for i in range(owners)
        ]

    chain = [(i, next_on_chain(i)) for i in range(owners)]
    straight = to_next_section(lambda i: i)
    slanted = to_next_section(next_on_chain)
    first_section = lax.axis_index("sec") == 0

    swap = lambda value: lax.ppermute(value, "own", partner)
    pass_on = lambda value: lax.ppermute(value, "own", chain)
    section_hop = lambda value, pairs: lax.ppermute(value, ("sec", "own"), pairs)

    ticks, width, _ = right_sides.shape
    rows = width // STREAMS
    streams = range(STREAMS)
    solved_all = []
    for tick in range(ticks):
        if tick == 0:
            fixed, solved, lhs, early, keep4 = first_step(
                chips,
                STREAMS,
                rows,
                (ancestor, structure, right_sides, carried, inv_diag, factor_tiles),
            )
            solved_all.append(solved)
            early = [swap(value) for value in early]
            parts = late_step(chips, STREAMS, fixed, lhs)
            late = [swap(part[0]) for part in parts]
            keep = [part[1:] for part in parts]
        else:
            early, late, keep, keep4 = [], [], [], []
            for stream in streams:
                solved, lhs, early_one, keep4_one = next_step(
                    chips, tick, stream * rows, fixed, right_sides,
                    moving[stream], own, crossed[stream],
                )
                solved_all.append(solved)
                early.append(swap(early_one))
                keep4.append(keep4_one)
                late_one, *keep_one = late_step(chips, 1, fixed, lhs)[0]
                late.append(swap(late_one))
                keep.append(keep_one)
        moving, crossed, owns = [], [], []
        for stream in streams:
            keep3, keep2, keep1, keep0 = keep[stream]
            value = pass_on(keep4[stream] + early[stream][0])
            value = jnp.stack(
                [keep3[0] + early[stream][1] + value, keep3[1] + early[stream][2]]
            )
            value = pass_on(value)
            value = pass_on(keep2 + late[stream][0:2] + value)
            value = section_hop(keep1 + late[stream][2:4] + value, slanted)
            moving.append(value)
            crossed.append(swap(value[1]))
            owns.append(keep0 + late[stream][4])
        own = section_hop(jnp.concatenate(owns, axis=0), straight)
    carry = jnp.concatenate([value[0] for value in moving], axis=0) + own
    carry = jnp.where(first_section, 0.0, carry + jnp.concatenate(crossed, axis=0))
    return jnp.concatenate(solved_all, axis=0).reshape(right_sides.shape), carry


def solution(mesh):
    in_specs = (
        P(None, None, ("sec", "own")),
        P(("sec", "own"), None),
        P(("sec", "own"), None),
        P(("sec", "own"), None),
        P("sec", None),
        P(None, ("sec", "own")),
    )
    out_specs = (P(None, None, ("sec", "own")), P(None, ("sec", "own")))
    return jax.shard_map(
        shards, mesh=mesh, in_specs=in_specs, out_specs=out_specs, check_vma=False
    )
```

```python
import functools

import jax
import jax.numpy as jnp
from jax import lax
from jax.experimental import pallas as pl
from jax.experimental.pallas import tpu as pltpu
from jax.sharding import PartitionSpec as P


STREAMS = 2


def split(value):
    high = value.astype(jnp.bfloat16)
    return high, (value - high.astype(jnp.float32)).astype(jnp.bfloat16)


def dot(a, b):
    return jnp.dot(a, b, preferred_element_type=jnp.float32)


def product(table, lhs, factor, place, distance, to_core):
    chips, chip = place
    rows, block = lhs.shape[0] // 2, lhs.shape[1]
    target = ((chip + distance + chips) % chips) * 2 + to_core
    start = pl.multiple_of(table[0, target] * block, block)
    both = dot(lhs, factor[:, pl.ds(start, block)])
    return (both[:rows] + both[rows:]) * table[1, target].astype(jnp.float32)


def position(chips):
    me = lax.axis_index("own")
    chip, core = me // 2, me % 2
    return (chips, chip), core, 1 - 2 * ((chip + core) % 2)


def solve(residual, inverse_high, inverse_low):
    rows = residual.shape[0]
    high, low = split(residual)
    both = dot(jnp.concatenate([high, low], axis=0), inverse_high)
    result = both[:rows] + both[rows:] + dot(high, inverse_low)
    return result, jnp.concatenate(split(result), axis=0)


def parts_of_step(chips, step):
    _, core, ahead = position(chips)
    last = chips // 2 - 1 - step
    up, down = last, -last - 1
    mine = jnp.where(ahead == 1, up, down)
    other = up + down - mine
    for give, distance, first in (
        (True, other, (core + 1 + other) % 2),
        (False, mine, (core + mine) % 2),
    ):
        yield give, 0, distance, (first + 2) % 2
        yield give, 1, distance, (3 - first) % 2


def put_step(table, lhs, factor, chips, step, give, keep, offset):
    rows = keep[0].shape[1]
    place = position(chips)[0]
    for given, index, distance, to_core in parts_of_step(chips, step):
        whole = product(table, lhs, factor, place, distance, to_core)
        for stream, ref in enumerate(give if given else keep):
            ref[offset + index] = whole[stream * rows : (stream + 1) * rows]


def first_kernel(
    chips, streams, ancestor, structure, right_sides, carried, inverse, factor,
    table, factor_here, inverse_high, inverse_low, solved, lhs, *rest,
):
    early, keep = rest[:streams], rest[streams : 2 * streams]
    slots, present, right_here, carried_here, inverse_here, sems = rest[2 * streams :]
    copies = [
        pltpu.make_async_copy(source, target, sems.at[i])
        for i, (source, target) in enumerate(
            (
                (inverse, inverse_here),
                (right_sides.at[0], right_here),
                (carried, carried_here),
                (ancestor, slots),
                (structure, present),
                (factor, factor_here),
            )
        )
    ]
    for copy in copies:
        copy.start()
    for copy in copies[:3]:
        copy.wait()
    inverse_high[...], inverse_low[...] = split(inverse_here[...])
    solved[...], lhs[...] = solve(
        right_here[...] - carried_here[...], inverse_high[...], inverse_low[...]
    )
    copies[3].wait()
    copies[4].wait()
    for slot in range(slots.shape[1]):
        table[0, slots[0, slot]] = slot
        table[1, slots[0, slot]] = present[0, slot]
    copies[5].wait()
    put_step(table, lhs[...], factor_here, chips, 0, early, keep, 0)


def next_kernel(
    chips, tick, first_row, table, right_sides, moving, crossed,
    inverse_high, inverse_low, factor, solved, lhs, early, keep,
):
    here = pl.ds(first_row, solved.shape[0])
    incoming = moving[0] + crossed[...]
    incoming = jnp.where(lax.axis_index("sec") == 0, 0.0, incoming)
    solved[...], lhs[...] = solve(
        right_sides[tick, here] - incoming, inverse_high[...], inverse_low[...]
    )
    put_step(table, lhs[...], factor, chips, 0, [early], [keep], 0)


def late_kernel(chips, streams, table, lhs, factor, *outs):
    give, keep = outs[:streams], outs[streams:]
    value = lhs[...]
    for step in range(1, chips // 2):
        put_step(table, value, factor, chips, step, give, keep, 2 * (step - 1))


VMEM = pl.BlockSpec(memory_space=pltpu.VMEM)
SMEM = pl.BlockSpec(memory_space=pltpu.SMEM)
HBM = pl.BlockSpec(memory_space=pltpu.HBM)
F32 = functools.partial(jax.ShapeDtypeStruct, dtype=jnp.float32)
BF16 = functools.partial(jax.ShapeDtypeStruct, dtype=jnp.bfloat16)


def call(kernel, products, in_specs, outs, limit, scratch=()):
    return pl.pallas_call(
        kernel,
        out_shape=outs,
        in_specs=in_specs,
        out_specs=[SMEM if out.dtype == jnp.int32 else VMEM for out in outs],
        scratch_shapes=list(scratch),
        compiler_params=pltpu.CompilerParams(vmem_limit_bytes=limit << 20),
        cost_estimate=pl.CostEstimate(
            flops=products * 2 * 256 * 256 * 256,
            bytes_accessed=products * 65536 * 2,
            transcendentals=0,
        ),
    )


def first_step(chips, streams, rows, arrays):
    ancestor, _, _, carried, _, factor = arrays
    slots = ancestor.shape[1]
    width, block = carried.shape
    square = (block, block)
    outs = [jax.ShapeDtypeStruct((2, slots), jnp.int32), BF16(factor.shape)]
    outs += [BF16(square)] * 2 + [F32((width, block)), BF16((2 * width, block))]
    outs += [F32((2, rows, block))] * (2 * streams)
    scratch = [
        pltpu.SMEM((1, slots), jnp.int32),
        pltpu.SMEM((1, slots), jnp.int32),
        pltpu.VMEM((width, block), jnp.float32),
        pltpu.VMEM((width, block), jnp.float32),
        pltpu.VMEM(square, jnp.float32),
        pltpu.SemaphoreType.DMA((6,)),
    ]
    kernel = functools.partial(first_kernel, chips, streams)
    out = call(kernel, 6, [HBM] * 6, outs, 4, scratch)(
        *[pltpu.with_memory_space_constraint(array, pltpu.HBM) for array in arrays]
    )
    fixed, (solved, lhs) = out[:4], out[4:6]
    return fixed, solved, lhs, out[6 : 6 + streams], out[6 + streams :]


def next_step(chips, tick, first_row, fixed, right_sides, moving, crossed):
    table, factor, inverse_high, inverse_low = fixed
    rows, block = crossed.shape
    outs = [F32((rows, block)), BF16((2 * rows, block))]
    outs += [F32((2, rows, block))] * 2
    kernel = functools.partial(next_kernel, chips, tick, first_row)
    return call(kernel, 6, [SMEM] + [VMEM] * 6, outs, 4)(
        table, right_sides, moving, crossed, inverse_high, inverse_low, factor
    )


def late_step(chips, streams, fixed, lhs):
    rows, block = lhs.shape[0] // 2 // streams, lhs.shape[1]
    outs = [F32((chips - 2, rows, block))] * (2 * streams)
    kernel = functools.partial(late_kernel, chips, streams)
    out = call(kernel, 12, [SMEM, VMEM, VMEM], outs, 4)(fixed[0], lhs, fixed[1])
    return out[:streams], out[streams:]


def shards(right_sides, inv_diag, factor_tiles, structure, ancestor, carried):
    owners = lax.axis_size("own")
    sections = lax.axis_size("sec")
    chips = owners // 2
    partner = [(i, i ^ 1) for i in range(owners)]

    def next_on_chain(i):
        chip, core = i // 2, i % 2
        ahead = 1 - 2 * ((chip + core) % 2)
        return ((chip + ahead) % chips) * 2 + 1 - core

    def to_next_section(place):
        return [
            (s * owners + i, (s + 1) % sections * owners + place(i))
            for s in range(sections)
            for i in range(owners)
        ]

    chain = [(i, next_on_chain(i)) for i in range(owners)]
    upward = lambda i: (i // 2 + i) % 2 == 0
    onward = to_next_section(lambda i: i if upward(i) else next_on_chain(i))
    first_section = lax.axis_index("sec") == 0

    swap = lambda value: lax.ppermute(value, "own", partner)
    pass_on = lambda value: lax.ppermute(value, "own", chain)
    leave = lambda value: lax.ppermute(value, ("sec", "own"), onward)

    ticks, width, _ = right_sides.shape
    rows = width // STREAMS
    streams = range(STREAMS)
    solved_all = []
    for tick in range(ticks):
        if tick == 0:
            fixed, solved, lhs, gives, keeps = first_step(
                chips,
                STREAMS,
                rows,
                (ancestor, structure, right_sides, carried, inv_diag, factor_tiles),
            )
            solved_all.append(solved)
            later_gives, later_keeps = late_step(chips, STREAMS, fixed, lhs)
        else:
            gives, keeps, later_gives, later_keeps = [], [], [], []
            for stream in streams:
                solved, lhs, give, keep = next_step(
                    chips, tick, stream * rows, fixed, right_sides,
                    moving[stream], crossed[stream],
                )
                solved_all.append(solved)
                gives.append(give)
                keeps.append(keep)
                give, keep = late_step(chips, 1, fixed, lhs)
                later_gives += give
                later_keeps += keep
        moving, crossed = [], []
        for stream in streams:
            taken = swap(gives[stream])
            later = swap(later_gives[stream])
            value = keeps[stream] + taken
            for step in range(chips // 2 - 1):
                value = pass_on(value)
                part = slice(2 * step, 2 * step + 2)
                value = later_keeps[stream][part] + later[part] + value
            value = leave(value)
            moving.append(value)
            crossed.append(swap(value[1]))
    carry = jnp.concatenate([value[0] for value in moving], axis=0)
    carry = jnp.where(first_section, 0.0, carry + jnp.concatenate(crossed, axis=0))
    return jnp.concatenate(solved_all, axis=0).reshape(right_sides.shape), carry


def solution(mesh):
    in_specs = (
        P(None, None, ("sec", "own")),
        P(("sec", "own"), None),
        P(("sec", "own"), None),
        P(("sec", "own"), None),
        P("sec", None),
        P(None, ("sec", "own")),
    )
    out_specs = (P(None, None, ("sec", "own")), P(None, ("sec", "own")))
    return jax.shard_map(
        shards,
        mesh=mesh,
        in_specs=in_specs,
        out_specs=out_specs,
        check_vma=False,
    )
```

```python
import functools

import jax
import jax.numpy as jnp
from jax import lax
from jax.experimental import pallas as pl
from jax.experimental.pallas import tpu as pltpu
from jax.sharding import PartitionSpec as P


STREAMS = 2


def split(value):
    high = value.astype(jnp.bfloat16)
    return high, (value - high.astype(jnp.float32)).astype(jnp.bfloat16)


def dot(a, b):
    return jnp.dot(a, b, preferred_element_type=jnp.float32)


def blocks_of(chips, core, chip, names):
    ahead = 1 - 2 * ((chip + core) % 2)
    for name in names:
        if name == "far":
            yield chips // 2, core
        elif name == "own":
            yield 0, 1 - core
        else:
            first = (core + name) % 2
            yield name * ahead, first
            yield name * ahead, 1 - first


EARLY = (3, "far", "own")
LATE = (2, 1)


def put(table, lhs, factor, chips, names, gives, keeps):
    rows, block = gives[0].shape[1:]
    me = lax.axis_index("own")
    chip, core = me // 2, me % 2
    for refs, who in ((gives, 1 - core), (keeps, core)):
        for place, (distance, to_core) in enumerate(blocks_of(chips, who, chip, names)):
            target = (chip + distance + chips) % chips * 2 + to_core
            start = pl.multiple_of(table[0, target] * block, block)
            both = dot(lhs, factor[:, pl.ds(start, block)])
            scale = table[1, target].astype(jnp.float32)
            for stream, ref in enumerate(refs):
                low = slice((2 * stream + 1) * rows, (2 * stream + 2) * rows)
                high = slice(2 * stream * rows, (2 * stream + 1) * rows)
                ref[place] = (both[high] + both[low]) * scale


def solve(residual, inverse_high, inverse_low, streams):
    width = residual.shape[0]
    rows = width // streams
    high, low = split(residual)
    both = dot(jnp.concatenate([high, low], axis=0), inverse_high)
    result = both[:width] + both[width:] + dot(high, inverse_low)
    high, low = split(result)
    parts = []
    for stream in range(streams):
        here = slice(stream * rows, (stream + 1) * rows)
        parts += [high[here], low[here]]
    return result, jnp.concatenate(parts, axis=0)


def first_kernel(
    chips, streams, ancestor, structure, right_sides, carried, inverse, factor,
    table, factor_here, inverse_high, inverse_low, solved, lhs, *rest,
):
    gives, keeps = rest[:streams], rest[streams : 2 * streams]
    slots, present, right_here, carried_here, inverse_here, sems = rest[2 * streams :]
    chunk = factor.shape[0] // 4
    pairs = [
        (inverse, inverse_here),
        (right_sides.at[0], right_here),
        (carried, carried_here),
        (ancestor, slots),
        (structure, present),
    ]
    for i in range(4):
        here = pl.ds(i * chunk, chunk)
        pairs.append((factor.at[here], factor_here.at[here]))
    copies = [
        pltpu.make_async_copy(source, target, sems.at[i])
        for i, (source, target) in enumerate(pairs)
    ]
    for copy in copies:
        copy.start()
    for copy in copies[:3]:
        copy.wait()
    inverse_high[...], inverse_low[...] = split(inverse_here[...])
    solved[...], lhs[...] = solve(
        right_here[...] - carried_here[...], inverse_high[...], inverse_low[...], streams
    )
    copies[3].wait()
    copies[4].wait()
    for slot in range(slots.shape[1]):
        table[0, slots[0, slot]] = slot
        table[1, slots[0, slot]] = present[0, slot]
    for copy in copies[5:]:
        copy.wait()
    put(table, lhs[...], factor_here, chips, EARLY, gives, keeps)


def next_kernel(
    chips, tick, first_row, table, right_sides, moving, crossed,
    inverse_high, inverse_low, factor, solved, lhs, give, keep,
):
    here = pl.ds(first_row, solved.shape[0])
    incoming = moving[0] + crossed[...]
    incoming = jnp.where(lax.axis_index("sec") == 0, 0.0, incoming)
    solved[...], lhs[...] = solve(
        right_sides[tick, here] - incoming, inverse_high[...], inverse_low[...], 1
    )
    put(table, lhs[...], factor, chips, EARLY, [give], [keep])


def late_kernel(chips, streams, table, factor, *rest):
    parts, outs = rest[: -2 * streams], rest[-2 * streams :]
    lhs = jnp.concatenate([part[...] for part in parts], axis=0)
    put(table, lhs, factor, chips, LATE, outs[:streams], outs[streams:])


VMEM = pl.BlockSpec(memory_space=pltpu.VMEM)
SMEM = pl.BlockSpec(memory_space=pltpu.SMEM)
HBM = pl.BlockSpec(memory_space=pltpu.HBM)
F32 = functools.partial(jax.ShapeDtypeStruct, dtype=jnp.float32)
BF16 = functools.partial(jax.ShapeDtypeStruct, dtype=jnp.bfloat16)


def call(kernel, products, in_specs, outs, limit, scratch=()):
    return pl.pallas_call(
        kernel,
        out_shape=outs,
        in_specs=in_specs,
        out_specs=[SMEM if out.dtype == jnp.int32 else VMEM for out in outs],
        scratch_shapes=list(scratch),
        compiler_params=pltpu.CompilerParams(vmem_limit_bytes=limit << 20),
        cost_estimate=pl.CostEstimate(
            flops=products * 2 * 256 * 256 * 256,
            bytes_accessed=products * 65536 * 2,
            transcendentals=0,
        ),
    )


def first_step(chips, streams, rows, arrays):
    ancestor, _, _, carried, _, factor = arrays
    slots = ancestor.shape[1]
    width, block = carried.shape
    square = (block, block)
    outs = [jax.ShapeDtypeStruct((2, slots), jnp.int32), BF16(factor.shape)]
    outs += [BF16(square)] * 2 + [F32((width, block)), BF16((2 * width, block))]
    outs += [F32((4, rows, block))] * (2 * streams)
    scratch = [
        pltpu.SMEM((1, slots), jnp.int32),
        pltpu.SMEM((1, slots), jnp.int32),
        pltpu.VMEM((width, block), jnp.float32),
        pltpu.VMEM((width, block), jnp.float32),
        pltpu.VMEM(square, jnp.float32),
        pltpu.SemaphoreType.DMA((9,)),
    ]
    kernel = functools.partial(first_kernel, chips, streams)
    out = call(kernel, 6, [HBM] * 6, outs, 4, scratch)(
        *[pltpu.with_memory_space_constraint(array, pltpu.HBM) for array in arrays]
    )
    fixed, (solved, lhs) = out[:4], out[4:6]
    return fixed, solved, lhs, out[6 : 6 + streams], out[6 + streams :]


def next_step(chips, tick, first_row, fixed, right_sides, moving, crossed):
    table, factor, inverse_high, inverse_low = fixed
    rows, block = crossed.shape
    outs = [F32((rows, block)), BF16((2 * rows, block))]
    outs += [F32((4, rows, block))] * 2
    kernel = functools.partial(next_kernel, chips, tick, first_row)
    return call(kernel, 6, [SMEM] + [VMEM] * 6, outs, 4)(
        table, right_sides, moving, crossed, inverse_high, inverse_low, factor
    )


def late_step(chips, streams, fixed, parts):
    block = parts[0].shape[1]
    rows = sum(part.shape[0] for part in parts) // 2 // streams
    outs = [F32((4, rows, block))] * (2 * streams)
    kernel = functools.partial(late_kernel, chips, streams)
    out = call(kernel, 16, [SMEM] + [VMEM] * (1 + len(parts)), outs, 4)(
        fixed[0], fixed[1], *parts
    )
    return out[:streams], out[streams:]


def shards(right_sides, inv_diag, factor_tiles, structure, ancestor, carried):
    owners = lax.axis_size("own")
    sections = lax.axis_size("sec")
    chips = owners // 2
    partner = [(i, i ^ 1) for i in range(owners)]

    def next_on_chain(i):
        chip, core = i // 2, i % 2
        ahead = 1 - 2 * ((chip + core) % 2)
        return ((chip + ahead) % chips) * 2 + 1 - core

    def to_next_section(place):
        return [
            (s * owners + i, (s + 1) % sections * owners + place(i))
            for s in range(sections)
            for i in range(owners)
        ]

    chain = [(i, next_on_chain(i)) for i in range(owners)]
    slanted = to_next_section(next_on_chain)
    first_section = lax.axis_index("sec") == 0

    def on_chain(chips_on):
        pairs = []
        for i in range(owners):
            ahead = 1 - 2 * ((i // 2 + i) % 2)
            pairs.append((i, (i // 2 + chips_on * ahead) % chips * 2 + 1 - i % 2))
        return pairs

    own_permute = lambda value, pairs: lax.ppermute(value, "own", pairs)
    swap = lambda value: own_permute(value, partner)

    ticks, width, _ = right_sides.shape
    rows = width // STREAMS
    streams = range(STREAMS)
    solved_all = []
    for tick in range(ticks):
        if tick == 0:
            fixed, solved, lhs, gives, keeps = first_step(
                chips,
                STREAMS,
                rows,
                (ancestor, structure, right_sides, carried, inv_diag, factor_tiles),
            )
            solved_all.append(solved)
            parts = [lhs]
        else:
            gives, keeps, parts = [], [], []
            for stream in streams:
                solved, lhs, give, keep = next_step(
                    chips, tick, stream * rows, fixed, right_sides,
                    moving[stream], crossed[stream],
                )
                solved_all.append(solved)
                gives.append(give)
                keeps.append(keep)
                parts.append(lhs)
        later_gives, later_keeps = late_step(chips, STREAMS, fixed, parts)
        sums = []
        for stream in streams:
            sums.append(keeps[stream] + swap(gives[stream]))
        far = jnp.concatenate([value[2] for value in sums], axis=0)
        own = jnp.concatenate([value[3] for value in sums], axis=0)
        far = own_permute(far, on_chain(chips // 2 - 1))
        own = own_permute(own, on_chain(-1))
        joining = jnp.stack([far, own])
        joining = lax.optimization_barrier(
            [joining[:, stream * rows : (stream + 1) * rows] for stream in streams]
        )
        moving, crossed = [], []
        for stream in streams:
            later = later_keeps[stream] + swap(later_gives[stream])
            value = own_permute(sums[stream][:2], chain)
            value = later[:2] + value
            value = own_permute(value, chain)
            value = later[2:] + joining[stream] + value
            value = lax.ppermute(value, ("sec", "own"), slanted)
            moving.append(value)
            crossed.append(swap(value[1]))
    carry = jnp.concatenate([value[0] for value in moving], axis=0)
    carry = jnp.where(first_section, 0.0, carry + jnp.concatenate(crossed, axis=0))
    return jnp.concatenate(solved_all, axis=0).reshape(right_sides.shape), carry


def solution(mesh):
    in_specs = (
        P(None, None, ("sec", "own")),
        P(("sec", "own"), None),
        P(("sec", "own"), None),
        P(("sec", "own"), None),
        P("sec", None),
        P(None, ("sec", "own")),
    )
    out_specs = (P(None, None, ("sec", "own")), P(None, ("sec", "own")))
    return jax.shard_map(
        shards,
        mesh=mesh,
        in_specs=in_specs,
        out_specs=out_specs,
        check_vma=False,
    )
```

```python
import functools

import jax
import jax.numpy as jnp
from jax import lax
from jax.experimental import pallas as pl
from jax.experimental.pallas import tpu as pltpu
from jax.sharding import PartitionSpec as P


STREAMS = 2


def split(value):
    high = value.astype(jnp.bfloat16)
    return high, (value - high.astype(jnp.float32)).astype(jnp.bfloat16)


def dot(a, b):
    return jnp.dot(a, b, preferred_element_type=jnp.float32)


def blocks_of(chips, core, chip, names):
    downward = (chip + core) % 2
    for name in names:
        if name == "side":
            first, distance = core, chips // 2 * (1 - downward)
        else:
            first, distance = (core + name) % 2, name * (1 - 2 * downward)
        yield distance, first
        yield distance, 1 - first


EARLY = (3, "side")
LATE = (2, 1)


def put(table, lhs, factor, chips, names, gives, keeps):
    rows, block = gives[0].shape[1:]
    me = lax.axis_index("own")
    chip, core = me // 2, me % 2
    for refs, who in ((gives, 1 - core), (keeps, core)):
        for place, (distance, to_core) in enumerate(blocks_of(chips, who, chip, names)):
            target = (chip + distance + chips) % chips * 2 + to_core
            start = pl.multiple_of(table[0, target] * block, block)
            both = dot(lhs, factor[:, pl.ds(start, block)])
            scale = table[1, target].astype(jnp.float32)
            for stream, ref in enumerate(refs):
                low = slice((2 * stream + 1) * rows, (2 * stream + 2) * rows)
                high = slice(2 * stream * rows, (2 * stream + 1) * rows)
                ref[place] = (both[high] + both[low]) * scale


def solve(residual, inverse_high, inverse_low, streams):
    width = residual.shape[0]
    rows = width // streams
    high, low = split(residual)
    both = dot(jnp.concatenate([high, low], axis=0), inverse_high)
    result = both[:width] + both[width:] + dot(high, inverse_low)
    high, low = split(result)
    parts = []
    for stream in range(streams):
        here = slice(stream * rows, (stream + 1) * rows)
        parts += [high[here], low[here]]
    return result, jnp.concatenate(parts, axis=0)


def first_kernel(
    chips, streams, ancestor, structure, right_sides, carried, inverse, factor,
    table, factor_here, inverse_high, inverse_low, solved, lhs, *rest,
):
    gives, keeps = rest[:streams], rest[streams : 2 * streams]
    slots, present, right_here, carried_here, inverse_here, sems = rest[2 * streams :]
    chunk = factor.shape[0] // 4
    pairs = [
        (inverse, inverse_here),
        (right_sides.at[0], right_here),
        (carried, carried_here),
        (ancestor, slots),
        (structure, present),
    ]
    for i in range(4):
        here = pl.ds(i * chunk, chunk)
        pairs.append((factor.at[here], factor_here.at[here]))
    copies = [
        pltpu.make_async_copy(source, target, sems.at[i])
        for i, (source, target) in enumerate(pairs)
    ]
    for copy in copies:
        copy.start()
    for copy in copies[:3]:
        copy.wait()
    inverse_high[...], inverse_low[...] = split(inverse_here[...])
    solved[...], lhs[...] = solve(
        right_here[...] - carried_here[...], inverse_high[...], inverse_low[...], streams
    )
    copies[3].wait()
    copies[4].wait()
    for slot in range(slots.shape[1]):
        table[0, slots[0, slot]] = slot
        table[1, slots[0, slot]] = present[0, slot]
    for copy in copies[5:]:
        copy.wait()
    put(table, lhs[...], factor_here, chips, EARLY, gives, keeps)


def next_kernel(
    chips, tick, first_row, table, right_sides, moving, crossed,
    inverse_high, inverse_low, factor, solved, lhs, give, keep,
):
    here = pl.ds(first_row, solved.shape[0])
    incoming = moving[0] + crossed[...]
    incoming = jnp.where(lax.axis_index("sec") == 0, 0.0, incoming)
    solved[...], lhs[...] = solve(
        right_sides[tick, here] - incoming, inverse_high[...], inverse_low[...], 1
    )
    put(table, lhs[...], factor, chips, EARLY, [give], [keep])


def late_kernel(chips, streams, table, factor, *rest):
    parts, outs = rest[: -2 * streams], rest[-2 * streams :]
    lhs = jnp.concatenate([part[...] for part in parts], axis=0)
    put(table, lhs, factor, chips, LATE, outs[:streams], outs[streams:])


VMEM = pl.BlockSpec(memory_space=pltpu.VMEM)
SMEM = pl.BlockSpec(memory_space=pltpu.SMEM)
HBM = pl.BlockSpec(memory_space=pltpu.HBM)
F32 = functools.partial(jax.ShapeDtypeStruct, dtype=jnp.float32)
BF16 = functools.partial(jax.ShapeDtypeStruct, dtype=jnp.bfloat16)


def call(kernel, products, in_specs, outs, limit, scratch=()):
    return pl.pallas_call(
        kernel,
        out_shape=outs,
        in_specs=in_specs,
        out_specs=[SMEM if out.dtype == jnp.int32 else VMEM for out in outs],
        scratch_shapes=list(scratch),
        compiler_params=pltpu.CompilerParams(vmem_limit_bytes=limit << 20),
        cost_estimate=pl.CostEstimate(
            flops=products * 2 * 256 * 256 * 256,
            bytes_accessed=products * 65536 * 2,
            transcendentals=0,
        ),
    )


def first_step(chips, streams, rows, arrays):
    ancestor, _, _, carried, _, factor = arrays
    slots = ancestor.shape[1]
    width, block = carried.shape
    square = (block, block)
    outs = [jax.ShapeDtypeStruct((2, slots), jnp.int32), BF16(factor.shape)]
    outs += [BF16(square)] * 2 + [F32((width, block)), BF16((2 * width, block))]
    outs += [F32((4, rows, block))] * (2 * streams)
    scratch = [
        pltpu.SMEM((1, slots), jnp.int32),
        pltpu.SMEM((1, slots), jnp.int32),
        pltpu.VMEM((width, block), jnp.float32),
        pltpu.VMEM((width, block), jnp.float32),
        pltpu.VMEM(square, jnp.float32),
        pltpu.SemaphoreType.DMA((9,)),
    ]
    kernel = functools.partial(first_kernel, chips, streams)
    out = call(kernel, 6, [HBM] * 6, outs, 4, scratch)(
        *[pltpu.with_memory_space_constraint(array, pltpu.HBM) for array in arrays]
    )
    fixed, (solved, lhs) = out[:4], out[4:6]
    return fixed, solved, lhs, out[6 : 6 + streams], out[6 + streams :]


def next_step(chips, tick, first_row, fixed, right_sides, moving, crossed):
    table, factor, inverse_high, inverse_low = fixed
    rows, block = crossed.shape
    outs = [F32((rows, block)), BF16((2 * rows, block))]
    outs += [F32((4, rows, block))] * 2
    kernel = functools.partial(next_kernel, chips, tick, first_row)
    return call(kernel, 6, [SMEM] + [VMEM] * 6, outs, 4)(
        table, right_sides, moving, crossed, inverse_high, inverse_low, factor
    )


def late_step(chips, streams, fixed, parts):
    block = parts[0].shape[1]
    rows = sum(part.shape[0] for part in parts) // 2 // streams
    outs = [F32((4, rows, block))] * (2 * streams)
    kernel = functools.partial(late_kernel, chips, streams)
    out = call(kernel, 16, [SMEM] + [VMEM] * (1 + len(parts)), outs, 4)(
        fixed[0], fixed[1], *parts
    )
    return out[:streams], out[streams:]


def shards(right_sides, inv_diag, factor_tiles, structure, ancestor, carried):
    owners = lax.axis_size("own")
    sections = lax.axis_size("sec")
    chips = owners // 2
    partner = [(i, i ^ 1) for i in range(owners)]

    def next_on_chain(i):
        chip, core = i // 2, i % 2
        ahead = 1 - 2 * ((chip + core) % 2)
        return ((chip + ahead) % chips) * 2 + 1 - core

    def to_next_section(place):
        return [
            (s * owners + i, (s + 1) % sections * owners + place(i))
            for s in range(sections)
            for i in range(owners)
        ]

    chain = [(i, next_on_chain(i)) for i in range(owners)]
    slanted = to_next_section(next_on_chain)
    first_section = lax.axis_index("sec") == 0

    def to_side(i):
        chip, core = i // 2, i % 2
        chips_on = 1 if (chip + core) % 2 else chips // 2 - 1
        return (chip + chips_on) % chips * 2 + 1 - core

    beside = [(i, to_side(i)) for i in range(owners)]
    own_permute = lambda value, pairs: lax.ppermute(value, "own", pairs)
    swap = lambda value: own_permute(value, partner)

    ticks, width, _ = right_sides.shape
    rows = width // STREAMS
    streams = range(STREAMS)
    solved_all = []
    for tick in range(ticks):
        if tick == 0:
            fixed, solved, lhs, gives, keeps = first_step(
                chips,
                STREAMS,
                rows,
                (ancestor, structure, right_sides, carried, inv_diag, factor_tiles),
            )
            solved_all.append(solved)
            parts = [lhs]
        else:
            gives, keeps, parts = [], [], []
            for stream in streams:
                solved, lhs, give, keep = next_step(
                    chips, tick, stream * rows, fixed, right_sides,
                    moving[stream], crossed[stream],
                )
                solved_all.append(solved)
                gives.append(give)
                keeps.append(keep)
                parts.append(lhs)
        later_gives, later_keeps = late_step(chips, STREAMS, fixed, parts)
        sums = []
        for stream in streams:
            sums.append(keeps[stream] + swap(gives[stream]))
        side = jnp.concatenate([value[2:] for value in sums], axis=1)
        side = own_permute(side, beside)
        joining = lax.optimization_barrier(
            [side[:, stream * rows : (stream + 1) * rows] for stream in streams]
        )
        moving, crossed = [], []
        for stream in streams:
            later = later_keeps[stream] + swap(later_gives[stream])
            value = own_permute(sums[stream][:2], chain)
            value = later[:2] + value
            value = own_permute(value, chain)
            value = later[2:] + joining[stream] + value
            value = lax.ppermute(value, ("sec", "own"), slanted)
            moving.append(value)
            crossed.append(swap(value[1]))
    carry = jnp.concatenate([value[0] for value in moving], axis=0)
    carry = jnp.where(first_section, 0.0, carry + jnp.concatenate(crossed, axis=0))
    return jnp.concatenate(solved_all, axis=0).reshape(right_sides.shape), carry


def solution(mesh):
    in_specs = (
        P(None, None, ("sec", "own")),
        P(("sec", "own"), None),
        P(("sec", "own"), None),
        P(("sec", "own"), None),
        P("sec", None),
        P(None, ("sec", "own")),
    )
    out_specs = (P(None, None, ("sec", "own")), P(None, ("sec", "own")))
    return jax.shard_map(
        shards,
        mesh=mesh,
        in_specs=in_specs,
        out_specs=out_specs,
        check_vma=False,
    )
```

```python
import functools

import jax
import jax.numpy as jnp
from jax import lax
from jax.experimental import pallas as pl
from jax.experimental.pallas import tpu as pltpu
from jax.sharding import PartitionSpec as P


STREAMS = 2


def split(value):
    high = value.astype(jnp.bfloat16)
    return high, (value - high.astype(jnp.float32)).astype(jnp.bfloat16)


def dot(a, b):
    return jnp.dot(a, b, preferred_element_type=jnp.float32)


def blocks_of(chips, core, chip, names):
    ahead = 1 - 2 * ((chip + core) % 2)
    for name in names:
        if name == "far":
            yield chips // 2, core
        elif name == "own":
            yield 0, 1 - core
        else:
            first = (core + name) % 2
            yield name * ahead, first
            yield name * ahead, 1 - first


EARLY = (3,)
SIDE = ("far", "own")
LATE = (2, 1)


def put(table, lhs, factor, chips, names, gives, keeps):
    rows, block = gives[0].shape[1:]
    me = lax.axis_index("own")
    chip, core = me // 2, me % 2
    for refs, who in ((gives, 1 - core), (keeps, core)):
        for place, (distance, to_core) in enumerate(blocks_of(chips, who, chip, names)):
            target = (chip + distance + chips) % chips * 2 + to_core
            start = pl.multiple_of(table[0, target] * block, block)
            both = dot(lhs, factor[:, pl.ds(start, block)])
            scale = table[1, target].astype(jnp.float32)
            for stream, ref in enumerate(refs):
                low = slice((2 * stream + 1) * rows, (2 * stream + 2) * rows)
                high = slice(2 * stream * rows, (2 * stream + 1) * rows)
                ref[place] = (both[high] + both[low]) * scale


def solve(residual, inverse_high, inverse_low, streams):
    width = residual.shape[0]
    rows = width // streams
    high, low = split(residual)
    both = dot(jnp.concatenate([high, low], axis=0), inverse_high)
    result = both[:width] + both[width:] + dot(high, inverse_low)
    high, low = split(result)
    parts = []
    for stream in range(streams):
        here = slice(stream * rows, (stream + 1) * rows)
        parts += [high[here], low[here]]
    return result, jnp.concatenate(parts, axis=0)


def first_kernel(
    chips, streams, ancestor, structure, right_sides, carried, inverse, factor,
    table, factor_here, inverse_high, inverse_low, solved, lhs, *rest,
):
    outs = [rest[i * streams : (i + 1) * streams] for i in range(4)]
    slots, present, right_here, carried_here, inverse_here, sems = rest[4 * streams :]
    chunk = factor.shape[0] // 4
    pairs = [
        (inverse, inverse_here),
        (right_sides.at[0], right_here),
        (carried, carried_here),
        (ancestor, slots),
        (structure, present),
    ]
    for i in range(4):
        here = pl.ds(i * chunk, chunk)
        pairs.append((factor.at[here], factor_here.at[here]))
    copies = [
        pltpu.make_async_copy(source, target, sems.at[i])
        for i, (source, target) in enumerate(pairs)
    ]
    for copy in copies:
        copy.start()
    for copy in copies[:3]:
        copy.wait()
    inverse_high[...], inverse_low[...] = split(inverse_here[...])
    solved[...], lhs[...] = solve(
        right_here[...] - carried_here[...], inverse_high[...], inverse_low[...], streams
    )
    copies[3].wait()
    copies[4].wait()
    for slot in range(slots.shape[1]):
        table[0, slots[0, slot]] = slot
        table[1, slots[0, slot]] = present[0, slot]
    for copy in copies[5:]:
        copy.wait()
    put(table, lhs[...], factor_here, chips, EARLY, *outs[:2])
    put(table, lhs[...], factor_here, chips, SIDE, *outs[2:])


def next_kernel(
    chips, tick, first_row, table, right_sides, moving, crossed,
    inverse_high, inverse_low, factor, solved, lhs, *outs,
):
    here = pl.ds(first_row, solved.shape[0])
    incoming = moving[0] + crossed[...]
    incoming = jnp.where(lax.axis_index("sec") == 0, 0.0, incoming)
    solved[...], lhs[...] = solve(
        right_sides[tick, here] - incoming, inverse_high[...], inverse_low[...], 1
    )
    outs = [[out] for out in outs]
    put(table, lhs[...], factor, chips, EARLY, *outs[:2])
    put(table, lhs[...], factor, chips, SIDE, *outs[2:])


def late_kernel(chips, streams, table, factor, *rest):
    parts, outs = rest[: -2 * streams], rest[-2 * streams :]
    lhs = jnp.concatenate([part[...] for part in parts], axis=0)
    put(table, lhs, factor, chips, LATE, outs[:streams], outs[streams:])


VMEM = pl.BlockSpec(memory_space=pltpu.VMEM)
SMEM = pl.BlockSpec(memory_space=pltpu.SMEM)
HBM = pl.BlockSpec(memory_space=pltpu.HBM)
F32 = functools.partial(jax.ShapeDtypeStruct, dtype=jnp.float32)
BF16 = functools.partial(jax.ShapeDtypeStruct, dtype=jnp.bfloat16)


def call(kernel, products, in_specs, outs, limit, scratch=()):
    return pl.pallas_call(
        kernel,
        out_shape=outs,
        in_specs=in_specs,
        out_specs=[SMEM if out.dtype == jnp.int32 else VMEM for out in outs],
        scratch_shapes=list(scratch),
        compiler_params=pltpu.CompilerParams(vmem_limit_bytes=limit << 20),
        cost_estimate=pl.CostEstimate(
            flops=products * 2 * 256 * 256 * 256,
            bytes_accessed=products * 65536 * 2,
            transcendentals=0,
        ),
    )


def first_step(chips, streams, rows, arrays):
    ancestor, _, _, carried, _, factor = arrays
    slots = ancestor.shape[1]
    width, block = carried.shape
    square = (block, block)
    outs = [jax.ShapeDtypeStruct((2, slots), jnp.int32), BF16(factor.shape)]
    outs += [BF16(square)] * 2 + [F32((width, block)), BF16((2 * width, block))]
    outs += [F32((2, rows, block))] * (4 * streams)
    scratch = [
        pltpu.SMEM((1, slots), jnp.int32),
        pltpu.SMEM((1, slots), jnp.int32),
        pltpu.VMEM((width, block), jnp.float32),
        pltpu.VMEM((width, block), jnp.float32),
        pltpu.VMEM(square, jnp.float32),
        pltpu.SemaphoreType.DMA((9,)),
    ]
    kernel = functools.partial(first_kernel, chips, streams)
    out = call(kernel, 6, [HBM] * 6, outs, 4, scratch)(
        *[pltpu.with_memory_space_constraint(array, pltpu.HBM) for array in arrays]
    )
    fixed, (solved, lhs) = out[:4], out[4:6]
    return fixed, solved, lhs, [out[i::streams] for i in range(6, 6 + streams)]


def next_step(chips, tick, first_row, fixed, right_sides, moving, crossed):
    table, factor, inverse_high, inverse_low = fixed
    rows, block = crossed.shape
    outs = [F32((rows, block)), BF16((2 * rows, block))]
    outs += [F32((2, rows, block))] * 4
    kernel = functools.partial(next_kernel, chips, tick, first_row)
    return call(kernel, 6, [SMEM] + [VMEM] * 6, outs, 4)(
        table, right_sides, moving, crossed, inverse_high, inverse_low, factor
    )


def late_step(chips, streams, fixed, parts):
    block = parts[0].shape[1]
    rows = sum(part.shape[0] for part in parts) // 2 // streams
    outs = [F32((4, rows, block))] * (2 * streams)
    kernel = functools.partial(late_kernel, chips, streams)
    out = call(kernel, 16, [SMEM] + [VMEM] * (1 + len(parts)), outs, 4)(
        fixed[0], fixed[1], *parts
    )
    return out[:streams], out[streams:]


def shards(right_sides, inv_diag, factor_tiles, structure, ancestor, carried):
    owners = lax.axis_size("own")
    sections = lax.axis_size("sec")
    chips = owners // 2
    partner = [(i, i ^ 1) for i in range(owners)]

    def next_on_chain(i):
        chip, core = i // 2, i % 2
        ahead = 1 - 2 * ((chip + core) % 2)
        return ((chip + ahead) % chips) * 2 + 1 - core

    def to_next_section(place):
        return [
            (s * owners + i, (s + 1) % sections * owners + place(i))
            for s in range(sections)
            for i in range(owners)
        ]

    chain = [(i, next_on_chain(i)) for i in range(owners)]
    slanted = to_next_section(next_on_chain)
    first_section = lax.axis_index("sec") == 0

    def on_chain(chips_on):
        pairs = []
        for i in range(owners):
            ahead = 1 - 2 * ((i // 2 + i) % 2)
            pairs.append((i, (i // 2 + chips_on * ahead) % chips * 2 + 1 - i % 2))
        return pairs

    own_permute = lambda value, pairs: lax.ppermute(value, "own", pairs)
    swap = lambda value: own_permute(value, partner)

    ticks, width, _ = right_sides.shape
    rows = width // STREAMS
    streams = range(STREAMS)
    solved_all = []
    for tick in range(ticks):
        if tick == 0:
            fixed, solved, lhs, outs = first_step(
                chips,
                STREAMS,
                rows,
                (ancestor, structure, right_sides, carried, inv_diag, factor_tiles),
            )
            solved_all.append(solved)
            parts = [lhs]
        else:
            outs, parts = [], []
            for stream in streams:
                solved, lhs, *out = next_step(
                    chips, tick, stream * rows, fixed, right_sides,
                    moving[stream], crossed[stream],
                )
                solved_all.append(solved)
                outs.append(out)
                parts.append(lhs)
        later_gives, later_keeps = late_step(chips, STREAMS, fixed, parts)
        sums, sides = [], []
        for stream in streams:
            give, keep, side_give, side_keep = outs[stream]
            sums.append(keep + swap(give))
            sides.append(side_keep + swap(side_give))
        far = jnp.concatenate([value[0] for value in sides], axis=0)
        own = jnp.concatenate([value[1] for value in sides], axis=0)
        far = own_permute(far, on_chain(chips // 2 - 1))
        own = own_permute(own, on_chain(-1))
        joining = jnp.stack([far, own])
        joining = lax.optimization_barrier(
            [joining[:, stream * rows : (stream + 1) * rows] for stream in streams]
        )
        moving, crossed = [], []
        for stream in streams:
            later = later_keeps[stream] + swap(later_gives[stream])
            value = own_permute(sums[stream], chain)
            value = later[:2] + value
            value = own_permute(value, chain)
            value = later[2:] + joining[stream] + value
            value = lax.ppermute(value, ("sec", "own"), slanted)
            moving.append(value)
            crossed.append(swap(value[1]))
    carry = jnp.concatenate([value[0] for value in moving], axis=0)
    carry = jnp.where(first_section, 0.0, carry + jnp.concatenate(crossed, axis=0))
    return jnp.concatenate(solved_all, axis=0).reshape(right_sides.shape), carry


def solution(mesh):
    in_specs = (
        P(None, None, ("sec", "own")),
        P(("sec", "own"), None),
        P(("sec", "own"), None),
        P(("sec", "own"), None),
        P("sec", None),
        P(None, ("sec", "own")),
    )
    out_specs = (P(None, None, ("sec", "own")), P(None, ("sec", "own")))
    return jax.shard_map(
        shards,
        mesh=mesh,
        in_specs=in_specs,
        out_specs=out_specs,
        check_vma=False,
    )
```

```python
import functools

import jax
import jax.numpy as jnp
from jax import lax
from jax.experimental import pallas as pl
from jax.experimental.pallas import tpu as pltpu
from jax.sharding import PartitionSpec as P


STREAMS = 2


def split(value):
    high = value.astype(jnp.bfloat16)
    return high, (value - high.astype(jnp.float32)).astype(jnp.bfloat16)


def dot(a, b):
    return jnp.dot(a, b, preferred_element_type=jnp.float32)


def product(table, lhs, factor, place, distance, to_core):
    chips, chip = place
    rows, block = lhs.shape[0] // 2, lhs.shape[1]
    target = ((chip + distance + chips) % chips) * 2 + to_core
    start = pl.multiple_of(table[0, target] * block, block)
    both = dot(lhs, factor[:, pl.ds(start, block)])
    return (both[:rows] + both[rows:]) * table[1, target].astype(jnp.float32)


def position(chips):
    me = lax.axis_index("own")
    chip, core = me // 2, me % 2
    return (chips, chip), core, 1 - 2 * ((chip + core) % 2)


def solve(residual, inverse_high, inverse_low):
    rows = residual.shape[0]
    high, low = split(residual)
    both = dot(jnp.concatenate([high, low], axis=0), inverse_high)
    result = both[:rows] + both[rows:] + dot(high, inverse_low)
    return result, jnp.concatenate(split(result), axis=0)


def parts_of_step(chips, step):
    _, core, ahead = position(chips)
    last = chips // 2 - 1 - step
    up, down = last, -last - 1
    mine = jnp.where(ahead == 1, up, down)
    other = up + down - mine
    for give, distance, first in (
        (True, other, (core + 1 + other) % 2),
        (False, mine, (core + mine) % 2),
    ):
        yield give, 0, distance, (first + 2) % 2
        yield give, 1, distance, (3 - first) % 2


def put_step(table, lhs, factor, chips, step, give, keep, offset):
    rows = keep[0].shape[1]
    place = position(chips)[0]
    for given, index, distance, to_core in parts_of_step(chips, step):
        whole = product(table, lhs, factor, place, distance, to_core)
        for stream, ref in enumerate(give if given else keep):
            ref[offset + index] = whole[stream * rows : (stream + 1) * rows]


def first_kernel(
    chips, streams, ancestor, structure, right_sides, carried, inverse, factor,
    table, factor_here, inverse_high, inverse_low, solved, lhs, *rest,
):
    early, keep = rest[:streams], rest[streams : 2 * streams]
    slots, present, right_here, carried_here, inverse_here, sems = rest[2 * streams :]
    copies = [
        pltpu.make_async_copy(source, target, sems.at[i])
        for i, (source, target) in enumerate(
            (
                (inverse, inverse_here),
                (right_sides.at[0], right_here),
                (carried, carried_here),
                (ancestor, slots),
                (structure, present),
                (factor, factor_here),
            )
        )
    ]
    for copy in copies:
        copy.start()
    for copy in copies[:3]:
        copy.wait()
    inverse_high[...], inverse_low[...] = split(inverse_here[...])
    solved[...], lhs[...] = solve(
        right_here[...] - carried_here[...], inverse_high[...], inverse_low[...]
    )
    copies[3].wait()
    copies[4].wait()
    for slot in range(slots.shape[1]):
        table[0, slots[0, slot]] = slot
        table[1, slots[0, slot]] = present[0, slot]
    copies[5].wait()
    put_step(table, lhs[...], factor_here, chips, 0, early, keep, 0)


def next_kernel(
    chips, tick, first_row, table, right_sides, moving, crossed,
    inverse_high, inverse_low, factor, solved, lhs, early, keep,
):
    here = pl.ds(first_row, solved.shape[0])
    incoming = moving[0] + crossed[...]
    incoming = jnp.where(lax.axis_index("sec") == 0, 0.0, incoming)
    solved[...], lhs[...] = solve(
        right_sides[tick, here] - incoming, inverse_high[...], inverse_low[...]
    )
    put_step(table, lhs[...], factor, chips, 0, [early], [keep], 0)


def late_kernel(chips, streams, table, factor, *rest):
    parts, outs = rest[: -2 * streams], rest[-2 * streams :]
    halves = [part.shape[0] // 2 for part in parts]
    highs = [part[:half] for part, half in zip(parts, halves)]
    lows = [part[half:] for part, half in zip(parts, halves)]
    lhs = jnp.concatenate(highs + lows, axis=0)
    for step in range(1, chips // 2):
        put_step(
            table, lhs, factor, chips, step,
            outs[:streams], outs[streams:], 2 * (step - 1),
        )


VMEM = pl.BlockSpec(memory_space=pltpu.VMEM)
SMEM = pl.BlockSpec(memory_space=pltpu.SMEM)
HBM = pl.BlockSpec(memory_space=pltpu.HBM)
F32 = functools.partial(jax.ShapeDtypeStruct, dtype=jnp.float32)
BF16 = functools.partial(jax.ShapeDtypeStruct, dtype=jnp.bfloat16)


def call(kernel, products, in_specs, outs, limit, scratch=()):
    return pl.pallas_call(
        kernel,
        out_shape=outs,
        in_specs=in_specs,
        out_specs=[SMEM if out.dtype == jnp.int32 else VMEM for out in outs],
        scratch_shapes=list(scratch),
        compiler_params=pltpu.CompilerParams(vmem_limit_bytes=limit << 20),
        cost_estimate=pl.CostEstimate(
            flops=products * 2 * 256 * 256 * 256,
            bytes_accessed=products * 65536 * 2,
            transcendentals=0,
        ),
    )


def first_step(chips, streams, rows, arrays):
    ancestor, _, _, carried, _, factor = arrays
    slots = ancestor.shape[1]
    width, block = carried.shape
    square = (block, block)
    outs = [jax.ShapeDtypeStruct((2, slots), jnp.int32), BF16(factor.shape)]
    outs += [BF16(square)] * 2 + [F32((width, block)), BF16((2 * width, block))]
    outs += [F32((2, rows, block))] * (2 * streams)
    scratch = [
        pltpu.SMEM((1, slots), jnp.int32),
        pltpu.SMEM((1, slots), jnp.int32),
        pltpu.VMEM((width, block), jnp.float32),
        pltpu.VMEM((width, block), jnp.float32),
        pltpu.VMEM(square, jnp.float32),
        pltpu.SemaphoreType.DMA((6,)),
    ]
    kernel = functools.partial(first_kernel, chips, streams)
    out = call(kernel, 6, [HBM] * 6, outs, 4, scratch)(
        *[pltpu.with_memory_space_constraint(array, pltpu.HBM) for array in arrays]
    )
    fixed, (solved, lhs) = out[:4], out[4:6]
    return fixed, solved, lhs, out[6 : 6 + streams], out[6 + streams :]


def next_step(chips, tick, first_row, fixed, right_sides, moving, crossed):
    table, factor, inverse_high, inverse_low = fixed
    rows, block = crossed.shape
    outs = [F32((rows, block)), BF16((2 * rows, block))]
    outs += [F32((2, rows, block))] * 2
    kernel = functools.partial(next_kernel, chips, tick, first_row)
    return call(kernel, 6, [SMEM] + [VMEM] * 6, outs, 4)(
        table, right_sides, moving, crossed, inverse_high, inverse_low, factor
    )


def late_step(chips, streams, fixed, parts):
    block = parts[0].shape[1]
    rows = sum(part.shape[0] for part in parts) // 2 // streams
    outs = [F32((chips - 2, rows, block))] * (2 * streams)
    kernel = functools.partial(late_kernel, chips, streams)
    out = call(kernel, 16, [SMEM] + [VMEM] * (1 + len(parts)), outs, 4)(
        fixed[0], fixed[1], *parts
    )
    return out[:streams], out[streams:]


def shards(right_sides, inv_diag, factor_tiles, structure, ancestor, carried):
    owners = lax.axis_size("own")
    sections = lax.axis_size("sec")
    chips = owners // 2
    partner = [(i, i ^ 1) for i in range(owners)]

    def next_on_chain(i):
        chip, core = i // 2, i % 2
        ahead = 1 - 2 * ((chip + core) % 2)
        return ((chip + ahead) % chips) * 2 + 1 - core

    def to_next_section(place):
        return [
            (s * owners + i, (s + 1) % sections * owners + place(i))
            for s in range(sections)
            for i in range(owners)
        ]

    chain = [(i, next_on_chain(i)) for i in range(owners)]
    upward = lambda i: (i // 2 + i) % 2 == 0
    onward = to_next_section(lambda i: i if upward(i) else next_on_chain(i))
    first_section = lax.axis_index("sec") == 0

    swap = lambda value: lax.ppermute(value, "own", partner)
    pass_on = lambda value: lax.ppermute(value, "own", chain)
    leave = lambda value: lax.ppermute(value, ("sec", "own"), onward)

    ticks, width, _ = right_sides.shape
    rows = width // STREAMS
    streams = range(STREAMS)
    solved_all = []
    for tick in range(ticks):
        if tick == 0:
            fixed, solved, lhs, gives, keeps = first_step(
                chips,
                STREAMS,
                rows,
                (ancestor, structure, right_sides, carried, inv_diag, factor_tiles),
            )
            solved_all.append(solved)
            parts = [lhs]
        else:
            gives, keeps, parts = [], [], []
            for stream in streams:
                solved, lhs, give, keep = next_step(
                    chips, tick, stream * rows, fixed, right_sides,
                    moving[stream], crossed[stream],
                )
                solved_all.append(solved)
                gives.append(give)
                keeps.append(keep)
                parts.append(lhs)
        later_gives, later_keeps = late_step(chips, STREAMS, fixed, parts)
        moving, crossed = [], []
        for stream in streams:
            taken = swap(gives[stream])
            later = swap(later_gives[stream])
            value = keeps[stream] + taken
            for step in range(chips // 2 - 1):
                value = pass_on(value)
                part = slice(2 * step, 2 * step + 2)
                value = later_keeps[stream][part] + later[part] + value
            value = leave(value)
            moving.append(value)
            crossed.append(swap(value[1]))
    carry = jnp.concatenate([value[0] for value in moving], axis=0)
    carry = jnp.where(first_section, 0.0, carry + jnp.concatenate(crossed, axis=0))
    return jnp.concatenate(solved_all, axis=0).reshape(right_sides.shape), carry


def solution(mesh):
    in_specs = (
        P(None, None, ("sec", "own")),
        P(("sec", "own"), None),
        P(("sec", "own"), None),
        P(("sec", "own"), None),
        P("sec", None),
        P(None, ("sec", "own")),
    )
    out_specs = (P(None, None, ("sec", "own")), P(None, ("sec", "own")))
    return jax.shard_map(
        shards,
        mesh=mesh,
        in_specs=in_specs,
        out_specs=out_specs,
        check_vma=False,
    )
```

```python
import functools

import jax
import jax.numpy as jnp
from jax import lax
from jax.experimental import pallas as pl
from jax.experimental.pallas import tpu as pltpu
from jax.sharding import PartitionSpec as P


STREAMS = 2


def split(value):
    high = value.astype(jnp.bfloat16)
    return high, (value - high.astype(jnp.float32)).astype(jnp.bfloat16)


def dot(a, b):
    return jnp.dot(a, b, preferred_element_type=jnp.float32)


def product(table, lhs, factor, place, distance, to_core):
    chips, chip = place
    rows, block = lhs.shape[0] // 2, lhs.shape[1]
    target = ((chip + distance + chips) % chips) * 2 + to_core
    start = pl.multiple_of(table[0, target] * block, block)
    both = dot(lhs, factor[:, pl.ds(start, block)])
    return (both[:rows] + both[rows:]) * table[1, target].astype(jnp.float32)


def position(chips):
    me = lax.axis_index("own")
    chip, core = me // 2, me % 2
    return (chips, chip), core, 1 - 2 * ((chip + core) % 2)


def solve(residual, inverse_high, inverse_low):
    rows = residual.shape[0]
    high, low = split(residual)
    both = dot(jnp.concatenate([high, low], axis=0), inverse_high)
    result = both[:rows] + both[rows:] + dot(high, inverse_low)
    return result, jnp.concatenate(split(result), axis=0)


def parts_of_step(chips, step):
    _, core, ahead = position(chips)
    last = chips // 2 - 1 - step
    up, down = last, -last - 1
    mine = jnp.where(ahead == 1, up, down)
    other = up + down - mine
    for give, distance, first in (
        (True, other, (core + 1 + other) % 2),
        (False, mine, (core + mine) % 2),
    ):
        yield give, 0, distance, (first + 2) % 2
        yield give, 1, distance, (3 - first) % 2


def put_step(table, lhs, factor, chips, step, give, keep, offset):
    rows = keep[0].shape[1]
    place = position(chips)[0]
    for given, index, distance, to_core in parts_of_step(chips, step):
        whole = product(table, lhs, factor, place, distance, to_core)
        for stream, ref in enumerate(give if given else keep):
            ref[offset + index] = whole[stream * rows : (stream + 1) * rows]


def first_kernel(
    chips, streams, ancestor, structure, right_sides, carried, inverse, factor,
    table, factor_here, inverse_high, inverse_low, solved, lhs, *rest,
):
    early, keep = rest[:streams], rest[streams : 2 * streams]
    slots, present, right_here, carried_here, inverse_here, sems = rest[2 * streams :]
    copies = [
        pltpu.make_async_copy(source, target, sems.at[i])
        for i, (source, target) in enumerate(
            (
                (inverse, inverse_here),
                (right_sides.at[0], right_here),
                (carried, carried_here),
                (ancestor, slots),
                (structure, present),
                (factor, factor_here),
            )
        )
    ]
    for copy in copies:
        copy.start()
    for copy in copies[:3]:
        copy.wait()
    inverse_high[...], inverse_low[...] = split(inverse_here[...])
    solved[...], lhs[...] = solve(
        right_here[...] - carried_here[...], inverse_high[...], inverse_low[...]
    )
    copies[3].wait()
    copies[4].wait()
    for slot in range(slots.shape[1]):
        table[0, slots[0, slot]] = slot
        table[1, slots[0, slot]] = present[0, slot]
    copies[5].wait()
    put_step(table, lhs[...], factor_here, chips, 0, early, keep, 0)


def next_kernel(
    chips, tick, first_row, table, right_sides, moving, crossed,
    inverse_high, inverse_low, factor, solved, lhs, early, keep,
):
    here = pl.ds(first_row, solved.shape[0])
    incoming = moving[0] + crossed[...]
    incoming = jnp.where(lax.axis_index("sec") == 0, 0.0, incoming)
    solved[...], lhs[...] = solve(
        right_sides[tick, here] - incoming, inverse_high[...], inverse_low[...]
    )
    put_step(table, lhs[...], factor, chips, 0, [early], [keep], 0)


def late_kernel(chips, streams, table, lhs, factor, *outs):
    give, keep = outs[:streams], outs[streams:]
    value = lhs[...]
    for step in range(1, chips // 2):
        put_step(table, value, factor, chips, step, give, keep, 2 * (step - 1))


VMEM = pl.BlockSpec(memory_space=pltpu.VMEM)
SMEM = pl.BlockSpec(memory_space=pltpu.SMEM)
HBM = pl.BlockSpec(memory_space=pltpu.HBM)
F32 = functools.partial(jax.ShapeDtypeStruct, dtype=jnp.float32)
BF16 = functools.partial(jax.ShapeDtypeStruct, dtype=jnp.bfloat16)


def call(kernel, products, in_specs, outs, limit, scratch=()):
    return pl.pallas_call(
        kernel,
        out_shape=outs,
        in_specs=in_specs,
        out_specs=[SMEM if out.dtype == jnp.int32 else VMEM for out in outs],
        scratch_shapes=list(scratch),
        compiler_params=pltpu.CompilerParams(vmem_limit_bytes=limit << 20),
        cost_estimate=pl.CostEstimate(
            flops=products * 2 * 256 * 256 * 256,
            bytes_accessed=products * 65536 * 2,
            transcendentals=0,
        ),
    )


def first_step(chips, streams, rows, arrays):
    ancestor, _, _, carried, _, factor = arrays
    slots = ancestor.shape[1]
    width, block = carried.shape
    square = (block, block)
    outs = [jax.ShapeDtypeStruct((2, slots), jnp.int32), BF16(factor.shape)]
    outs += [BF16(square)] * 2 + [F32((width, block)), BF16((2 * width, block))]
    outs += [F32((2, rows, block))] * (2 * streams)
    scratch = [
        pltpu.SMEM((1, slots), jnp.int32),
        pltpu.SMEM((1, slots), jnp.int32),
        pltpu.VMEM((width, block), jnp.float32),
        pltpu.VMEM((width, block), jnp.float32),
        pltpu.VMEM(square, jnp.float32),
        pltpu.SemaphoreType.DMA((6,)),
    ]
    kernel = functools.partial(first_kernel, chips, streams)
    out = call(kernel, 6, [HBM] * 6, outs, 4, scratch)(
        *[pltpu.with_memory_space_constraint(array, pltpu.HBM) for array in arrays]
    )
    fixed, (solved, lhs) = out[:4], out[4:6]
    return fixed, solved, lhs, out[6 : 6 + streams], out[6 + streams :]


def next_step(chips, tick, first_row, fixed, right_sides, moving, crossed):
    table, factor, inverse_high, inverse_low = fixed
    rows, block = crossed.shape
    outs = [F32((rows, block)), BF16((2 * rows, block))]
    outs += [F32((2, rows, block))] * 2
    kernel = functools.partial(next_kernel, chips, tick, first_row)
    return call(kernel, 6, [SMEM] + [VMEM] * 6, outs, 4)(
        table, right_sides, moving, crossed, inverse_high, inverse_low, factor
    )


def late_step(chips, streams, fixed, lhs):
    rows, block = lhs.shape[0] // 2 // streams, lhs.shape[1]
    outs = [F32((chips - 2, rows, block))] * (2 * streams)
    kernel = functools.partial(late_kernel, chips, streams)
    out = call(kernel, 12, [SMEM, VMEM, VMEM], outs, 4)(fixed[0], lhs, fixed[1])
    return out[:streams], out[streams:]


def shards(right_sides, inv_diag, factor_tiles, structure, ancestor, carried):
    owners = lax.axis_size("own")
    sections = lax.axis_size("sec")
    chips = owners // 2
    partner = [(i, i ^ 1) for i in range(owners)]

    def next_on_chain(i):
        chip, core = i // 2, i % 2
        ahead = 1 - 2 * ((chip + core) % 2)
        return ((chip + ahead) % chips) * 2 + 1 - core

    def to_next_section(place):
        last = sections - 1
        return [
            (s * owners + i, (s + 1) * owners + place(i))
            for s in range(last)
            for i in range(owners)
        ] + [(last * owners + i, i ^ 1) for i in range(owners)]

    chain = [(i, next_on_chain(i)) for i in range(owners)]
    upward = lambda i: (i // 2 + i) % 2 == 0
    onward = to_next_section(lambda i: i if upward(i) else next_on_chain(i))
    first_section = lax.axis_index("sec") == 0

    swap = lambda value: lax.ppermute(value, "own", partner)
    pass_on = lambda value: lax.ppermute(value, "own", chain)
    leave = lambda value: lax.ppermute(value, ("sec", "own"), onward)

    ticks, width, _ = right_sides.shape
    rows = width // STREAMS
    streams = range(STREAMS)
    solved_all = []
    for tick in range(ticks):
        if tick == 0:
            fixed, solved, lhs, gives, keeps = first_step(
                chips,
                STREAMS,
                rows,
                (ancestor, structure, right_sides, carried, inv_diag, factor_tiles),
            )
            solved_all.append(solved)
            later_gives, later_keeps = late_step(chips, STREAMS, fixed, lhs)
        else:
            gives, keeps, later_gives, later_keeps = [], [], [], []
            for stream in streams:
                solved, lhs, give, keep = next_step(
                    chips, tick, stream * rows, fixed, right_sides,
                    moving[stream], crossed[stream],
                )
                solved_all.append(solved)
                gives.append(give)
                keeps.append(keep)
                give, keep = late_step(chips, 1, fixed, lhs)
                later_gives += give
                later_keeps += keep
        moving, crossed = [], []
        for stream in streams:
            taken = swap(gives[stream])
            later = swap(later_gives[stream])
            value = keeps[stream] + taken
            for step in range(chips // 2 - 1):
                value = pass_on(value)
                part = slice(2 * step, 2 * step + 2)
                value = later_keeps[stream][part] + later[part] + value
            value = leave(value)
            moving.append(value)
            crossed.append(swap(value[1]))
    carry = jnp.concatenate([value[0] for value in moving], axis=0)
    carry = jnp.where(first_section, 0.0, carry + jnp.concatenate(crossed, axis=0))
    return jnp.concatenate(solved_all, axis=0).reshape(right_sides.shape), carry


def solution(mesh):
    in_specs = (
        P(None, None, ("sec", "own")),
        P(("sec", "own"), None),
        P(("sec", "own"), None),
        P(("sec", "own"), None),
        P("sec", None),
        P(None, ("sec", "own")),
    )
    out_specs = (P(None, None, ("sec", "own")), P(None, ("sec", "own")))
    return jax.shard_map(
        shards,
        mesh=mesh,
        in_specs=in_specs,
        out_specs=out_specs,
        check_vma=False,
    )
```

```python
import functools

import jax
import jax.numpy as jnp
from jax import lax
from jax.experimental import pallas as pl
from jax.experimental.pallas import tpu as pltpu
from jax.sharding import PartitionSpec as P


STREAMS = 2


def split(value):
    high = value.astype(jnp.bfloat16)
    return high, (value - high.astype(jnp.float32)).astype(jnp.bfloat16)


def dot(a, b):
    return jnp.dot(a, b, preferred_element_type=jnp.float32)


def product(table, lhs, factor, place, distance, to_core):
    chips, chip = place
    rows, block = lhs.shape[0] // 2, lhs.shape[1]
    target = ((chip + distance + chips) % chips) * 2 + to_core
    start = pl.multiple_of(table[0, target] * block, block)
    both = dot(lhs, factor[:, pl.ds(start, block)])
    return (both[:rows] + both[rows:]) * table[1, target].astype(jnp.float32)


def position(chips):
    me = lax.axis_index("own")
    chip, core = me // 2, me % 2
    return (chips, chip), core, 1 - 2 * ((chip + core) % 2)


def solve(residual, inverse_high, inverse_low):
    rows = residual.shape[0]
    high, low = split(residual)
    both = dot(jnp.concatenate([high, low], axis=0), inverse_high)
    result = both[:rows] + both[rows:] + dot(high, inverse_low)
    return result, jnp.concatenate(split(result), axis=0)


def parts_of_step(chips, step):
    _, core, ahead = position(chips)
    last = chips // 2 - 1 - step
    up, down = last, -last - 1
    mine = jnp.where(ahead == 1, up, down)
    other = up + down - mine
    for give, distance, first in (
        (True, other, (core + 1 + other) % 2),
        (False, mine, (core + mine) % 2),
    ):
        yield give, 0, distance, (first + 2) % 2
        yield give, 1, distance, (3 - first) % 2


def put_step(table, lhs, factor, chips, step, give, keep, offset):
    rows = keep[0].shape[1]
    place = position(chips)[0]
    for given, index, distance, to_core in parts_of_step(chips, step):
        whole = product(table, lhs, factor, place, distance, to_core)
        for stream, ref in enumerate(give if given else keep):
            ref[offset + index] = whole[stream * rows : (stream + 1) * rows]


def first_kernel(
    chips, streams, ancestor, structure, right_sides, carried, inverse, factor,
    table, factor_here, inverse_high, inverse_low, solved, lhs, *rest,
):
    early, keep = rest[:streams], rest[streams : 2 * streams]
    slots, present, right_here, carried_here, inverse_here, sems = rest[2 * streams :]
    copies = [
        pltpu.make_async_copy(source, target, sems.at[i])
        for i, (source, target) in enumerate(
            (
                (inverse, inverse_here),
                (right_sides.at[0], right_here),
                (carried, carried_here),
                (ancestor, slots),
                (structure, present),
                (factor, factor_here),
            )
        )
    ]
    for copy in copies:
        copy.start()
    for copy in copies[:3]:
        copy.wait()
    inverse_high[...], inverse_low[...] = split(inverse_here[...])
    solved[...], lhs[...] = solve(
        right_here[...] - carried_here[...], inverse_high[...], inverse_low[...]
    )
    copies[3].wait()
    copies[4].wait()
    for slot in range(slots.shape[1]):
        table[0, slots[0, slot]] = slot
        table[1, slots[0, slot]] = present[0, slot]
    copies[5].wait()
    put_step(table, lhs[...], factor_here, chips, 0, early, keep, 0)


def next_kernel(
    chips, tick, first_row, table, right_sides, moving, crossed,
    inverse_high, inverse_low, factor, solved, lhs, early, keep,
):
    here = pl.ds(first_row, solved.shape[0])
    incoming = moving[0] + crossed[...]
    incoming = jnp.where(lax.axis_index("sec") == 0, 0.0, incoming)
    solved[...], lhs[...] = solve(
        right_sides[tick, here] - incoming, inverse_high[...], inverse_low[...]
    )
    put_step(table, lhs[...], factor, chips, 0, [early], [keep], 0)


def late_kernel(chips, streams, table, factor, *rest):
    parts, outs = rest[: -2 * streams], rest[-2 * streams :]
    halves = [part.shape[0] // 2 for part in parts]
    highs = [part[:half] for part, half in zip(parts, halves)]
    lows = [part[half:] for part, half in zip(parts, halves)]
    lhs = jnp.concatenate(highs + lows, axis=0)
    for step in range(1, chips // 2):
        put_step(
            table, lhs, factor, chips, step,
            outs[:streams], outs[streams:], 2 * (step - 1),
        )


VMEM = pl.BlockSpec(memory_space=pltpu.VMEM)
SMEM = pl.BlockSpec(memory_space=pltpu.SMEM)
HBM = pl.BlockSpec(memory_space=pltpu.HBM)
F32 = functools.partial(jax.ShapeDtypeStruct, dtype=jnp.float32)
BF16 = functools.partial(jax.ShapeDtypeStruct, dtype=jnp.bfloat16)


def call(kernel, products, in_specs, outs, limit, scratch=()):
    return pl.pallas_call(
        kernel,
        out_shape=outs,
        in_specs=in_specs,
        out_specs=[SMEM if out.dtype == jnp.int32 else VMEM for out in outs],
        scratch_shapes=list(scratch),
        compiler_params=pltpu.CompilerParams(vmem_limit_bytes=limit << 20),
        cost_estimate=pl.CostEstimate(
            flops=products * 2 * 256 * 256 * 256,
            bytes_accessed=products * 65536 * 2,
            transcendentals=0,
        ),
    )


def first_step(chips, streams, rows, arrays):
    ancestor, _, _, carried, _, factor = arrays
    slots = ancestor.shape[1]
    width, block = carried.shape
    square = (block, block)
    outs = [jax.ShapeDtypeStruct((2, slots), jnp.int32), BF16(factor.shape)]
    outs += [BF16(square)] * 2 + [F32((width, block)), BF16((2 * width, block))]
    outs += [F32((2, rows, block))] * (2 * streams)
    scratch = [
        pltpu.SMEM((1, slots), jnp.int32),
        pltpu.SMEM((1, slots), jnp.int32),
        pltpu.VMEM((width, block), jnp.float32),
        pltpu.VMEM((width, block), jnp.float32),
        pltpu.VMEM(square, jnp.float32),
        pltpu.SemaphoreType.DMA((6,)),
    ]
    kernel = functools.partial(first_kernel, chips, streams)
    out = call(kernel, 6, [HBM] * 6, outs, 4, scratch)(
        *[pltpu.with_memory_space_constraint(array, pltpu.HBM) for array in arrays]
    )
    fixed, (solved, lhs) = out[:4], out[4:6]
    return fixed, solved, lhs, out[6 : 6 + streams], out[6 + streams :]


def next_step(chips, tick, first_row, fixed, right_sides, moving, crossed):
    table, factor, inverse_high, inverse_low = fixed
    rows, block = crossed.shape
    outs = [F32((rows, block)), BF16((2 * rows, block))]
    outs += [F32((2, rows, block))] * 2
    kernel = functools.partial(next_kernel, chips, tick, first_row)
    return call(kernel, 6, [SMEM] + [VMEM] * 6, outs, 4)(
        table, right_sides, moving, crossed, inverse_high, inverse_low, factor
    )


def late_step(chips, streams, fixed, parts):
    block = parts[0].shape[1]
    rows = sum(part.shape[0] for part in parts) // 2 // streams
    outs = [F32((chips - 2, rows, block))] * (2 * streams)
    kernel = functools.partial(late_kernel, chips, streams)
    out = call(kernel, 16, [SMEM] + [VMEM] * (1 + len(parts)), outs, 4)(
        fixed[0], fixed[1], *parts
    )
    return out[:streams], out[streams:]


def shards(right_sides, inv_diag, factor_tiles, structure, ancestor, carried):
    owners = lax.axis_size("own")
    sections = lax.axis_size("sec")
    chips = owners // 2
    partner = [(i, i ^ 1) for i in range(owners)]

    def next_on_chain(i):
        chip, core = i // 2, i % 2
        ahead = 1 - 2 * ((chip + core) % 2)
        return ((chip + ahead) % chips) * 2 + 1 - core

    def to_next_section(place):
        last = sections - 1
        return [
            (s * owners + i, (s + 1) * owners + place(i))
            for s in range(last)
            for i in range(owners)
        ] + [(last * owners + i, i ^ 1) for i in range(owners)]

    chain = [(i, next_on_chain(i)) for i in range(owners)]
    upward = lambda i: (i // 2 + i) % 2 == 0
    onward = to_next_section(lambda i: i if upward(i) else next_on_chain(i))
    first_section = lax.axis_index("sec") == 0

    swap = lambda value: lax.ppermute(value, "own", partner)
    pass_on = lambda value: lax.ppermute(value, "own", chain)
    leave = lambda value: lax.ppermute(value, ("sec", "own"), onward)

    ticks, width, _ = right_sides.shape
    rows = width // STREAMS
    streams = range(STREAMS)
    solved_all = []
    for tick in range(ticks):
        if tick == 0:
            fixed, solved, lhs, gives, keeps = first_step(
                chips,
                STREAMS,
                rows,
                (ancestor, structure, right_sides, carried, inv_diag, factor_tiles),
            )
            solved_all.append(solved)
            parts = [lhs]
        else:
            gives, keeps, parts = [], [], []
            for stream in streams:
                solved, lhs, give, keep = next_step(
                    chips, tick, stream * rows, fixed, right_sides,
                    moving[stream], crossed[stream],
                )
                solved_all.append(solved)
                gives.append(give)
                keeps.append(keep)
                parts.append(lhs)
        later_gives, later_keeps = late_step(chips, STREAMS, fixed, parts)
        moving, crossed = [], []
        for stream in streams:
            taken = swap(gives[stream])
            later = swap(later_gives[stream])
            value = keeps[stream] + taken
            for step in range(chips // 2 - 1):
                value = pass_on(value)
                part = slice(2 * step, 2 * step + 2)
                value = later_keeps[stream][part] + later[part] + value
            value = leave(value)
            moving.append(value)
            crossed.append(swap(value[1]))
    carry = jnp.concatenate([value[0] for value in moving], axis=0)
    carry = jnp.where(first_section, 0.0, carry + jnp.concatenate(crossed, axis=0))
    return jnp.concatenate(solved_all, axis=0).reshape(right_sides.shape), carry


def solution(mesh):
    in_specs = (
        P(None, None, ("sec", "own")),
        P(("sec", "own"), None),
        P(("sec", "own"), None),
        P(("sec", "own"), None),
        P("sec", None),
        P(None, ("sec", "own")),
    )
    out_specs = (P(None, None, ("sec", "own")), P(None, ("sec", "own")))
    return jax.shard_map(
        shards,
        mesh=mesh,
        in_specs=in_specs,
        out_specs=out_specs,
        check_vma=False,
    )
```

```python
import functools

import jax
import jax.numpy as jnp
from jax import lax
from jax.experimental import pallas as pl
from jax.experimental.pallas import tpu as pltpu
from jax.sharding import PartitionSpec as P


STREAMS = 1


def split(value):
    high = value.astype(jnp.bfloat16)
    return high, (value - high.astype(jnp.float32)).astype(jnp.bfloat16)


def dot(a, b):
    return jnp.dot(a, b, preferred_element_type=jnp.float32)


def product(table, lhs, factor, place, distance, to_core):
    chips, chip = place
    rows, block = lhs.shape[0] // 2, lhs.shape[1]
    target = ((chip + distance + chips) % chips) * 2 + to_core
    start = pl.multiple_of(table[0, target] * block, block)
    both = dot(lhs, factor[:, pl.ds(start, block)])
    return (both[:rows] + both[rows:]) * table[1, target].astype(jnp.float32)


def position(chips):
    me = lax.axis_index("own")
    chip, core = me // 2, me % 2
    return (chips, chip), core, 1 - 2 * ((chip + core) % 2)


def solve(residual, inverse_high, inverse_low):
    rows = residual.shape[0]
    high, low = split(residual)
    both = dot(jnp.concatenate([high, low], axis=0), inverse_high)
    result = both[:rows] + both[rows:] + dot(high, inverse_low)
    return result, jnp.concatenate(split(result), axis=0)


def parts_of_step(chips, step):
    _, core, ahead = position(chips)
    last = chips // 2 - 1 - step
    up, down = last, -last - 1
    mine = jnp.where(ahead == 1, up, down)
    other = up + down - mine
    for give, distance, first in (
        (True, other, (core + 1 + other) % 2),
        (False, mine, (core + mine) % 2),
    ):
        yield give, 0, distance, (first + 2) % 2
        yield give, 1, distance, (3 - first) % 2


def put_step(table, lhs, factor, chips, step, give, keep, offset):
    rows = keep[0].shape[1]
    place = position(chips)[0]
    for given, index, distance, to_core in parts_of_step(chips, step):
        whole = product(table, lhs, factor, place, distance, to_core)
        for stream, ref in enumerate(give if given else keep):
            ref[offset + index] = whole[stream * rows : (stream + 1) * rows]


def first_kernel(
    chips, streams, ancestor, structure, right_sides, carried, inverse, factor,
    table, factor_here, inverse_high, inverse_low, solved, lhs, *rest,
):
    early, keep = rest[:streams], rest[streams : 2 * streams]
    slots, present, right_here, carried_here, inverse_here, sems = rest[2 * streams :]
    copies = [
        pltpu.make_async_copy(source, target, sems.at[i])
        for i, (source, target) in enumerate(
            (
                (inverse, inverse_here),
                (right_sides.at[0], right_here),
                (carried, carried_here),
                (ancestor, slots),
                (structure, present),
                (factor, factor_here),
            )
        )
    ]
    for copy in copies:
        copy.start()
    for copy in copies[:3]:
        copy.wait()
    inverse_high[...], inverse_low[...] = split(inverse_here[...])
    solved[...], lhs[...] = solve(
        right_here[...] - carried_here[...], inverse_high[...], inverse_low[...]
    )
    copies[3].wait()
    copies[4].wait()
    for slot in range(slots.shape[1]):
        table[0, slots[0, slot]] = slot
        table[1, slots[0, slot]] = present[0, slot]
    copies[5].wait()
    put_step(table, lhs[...], factor_here, chips, 0, early, keep, 0)


def next_kernel(
    chips, streams, tick, table, right_sides, crossed,
    inverse_high, inverse_low, factor, *rest,
):
    moving, (solved, lhs), outs = rest[:streams], rest[streams : streams + 2], rest[streams + 2 :]
    incoming = jnp.concatenate([part[0] for part in moving], axis=0) + crossed[...]
    incoming = jnp.where(lax.axis_index("sec") == 0, 0.0, incoming)
    solved[...], lhs[...] = solve(
        right_sides[tick] - incoming, inverse_high[...], inverse_low[...]
    )
    put_step(table, lhs[...], factor, chips, 0, outs[:streams], outs[streams:], 0)


def late_kernel(chips, streams, table, factor, lhs, *outs):
    value = lhs[...]
    for step in range(1, chips // 2):
        put_step(
            table, value, factor, chips, step,
            outs[:streams], outs[streams:], 2 * (step - 1),
        )


VMEM = pl.BlockSpec(memory_space=pltpu.VMEM)
SMEM = pl.BlockSpec(memory_space=pltpu.SMEM)
HBM = pl.BlockSpec(memory_space=pltpu.HBM)
F32 = functools.partial(jax.ShapeDtypeStruct, dtype=jnp.float32)
BF16 = functools.partial(jax.ShapeDtypeStruct, dtype=jnp.bfloat16)


def call(kernel, products, in_specs, outs, limit, scratch=()):
    return pl.pallas_call(
        kernel,
        out_shape=outs,
        in_specs=in_specs,
        out_specs=[SMEM if out.dtype == jnp.int32 else VMEM for out in outs],
        scratch_shapes=list(scratch),
        compiler_params=pltpu.CompilerParams(vmem_limit_bytes=limit << 20),
        cost_estimate=pl.CostEstimate(
            flops=products * 2 * 256 * 256 * 256,
            bytes_accessed=products * 65536 * 2,
            transcendentals=0,
        ),
    )


def first_step(chips, streams, rows, arrays):
    ancestor, _, _, carried, _, factor = arrays
    slots = ancestor.shape[1]
    width, block = carried.shape
    square = (block, block)
    outs = [jax.ShapeDtypeStruct((2, slots), jnp.int32), BF16(factor.shape)]
    outs += [BF16(square)] * 2 + [F32((width, block)), BF16((2 * width, block))]
    outs += [F32((2, rows, block))] * (2 * streams)
    scratch = [
        pltpu.SMEM((1, slots), jnp.int32),
        pltpu.SMEM((1, slots), jnp.int32),
        pltpu.VMEM((width, block), jnp.float32),
        pltpu.VMEM((width, block), jnp.float32),
        pltpu.VMEM(square, jnp.float32),
        pltpu.SemaphoreType.DMA((6,)),
    ]
    kernel = functools.partial(first_kernel, chips, streams)
    out = call(kernel, 6, [HBM] * 6, outs, 4, scratch)(
        *[pltpu.with_memory_space_constraint(array, pltpu.HBM) for array in arrays]
    )
    fixed, (solved, lhs) = out[:4], out[4:6]
    return fixed, solved, lhs, out[6 : 6 + streams], out[6 + streams :]


def next_step(chips, tick, fixed, right_sides, moving, crossed):
    table, factor, inverse_high, inverse_low = fixed
    streams = len(moving)
    _, rows, block = moving[0].shape
    outs = [F32(crossed.shape), BF16((2 * streams * rows, block))]
    outs += [F32((2, rows, block))] * (2 * streams)
    kernel = functools.partial(next_kernel, chips, streams, tick)
    out = call(kernel, 6, [SMEM] + [VMEM] * (5 + streams), outs, 4)(
        table, right_sides, crossed, inverse_high, inverse_low, factor, *moving
    )
    return out[0], out[1], out[2 : 2 + streams], out[2 + streams :]


def late_step(chips, streams, fixed, lhs):
    rows, block = lhs.shape[0] // 2 // streams, lhs.shape[1]
    outs = [F32((chips - 2, rows, block))] * (2 * streams)
    kernel = functools.partial(late_kernel, chips, streams)
    out = call(kernel, 16, [SMEM, VMEM, VMEM], outs, 4)(fixed[0], fixed[1], lhs)
    return out[:streams], out[streams:]


def shards(right_sides, inv_diag, factor_tiles, structure, ancestor, carried):
    owners = lax.axis_size("own")
    sections = lax.axis_size("sec")
    chips = owners // 2
    partner = [(i, i ^ 1) for i in range(owners)]

    def next_on_chain(i):
        chip, core = i // 2, i % 2
        ahead = 1 - 2 * ((chip + core) % 2)
        return ((chip + ahead) % chips) * 2 + 1 - core

    def to_next_section(place):
        last = sections - 1
        return [
            (s * owners + i, (s + 1) * owners + place(i))
            for s in range(last)
            for i in range(owners)
        ] + [(last * owners + i, i ^ 1) for i in range(owners)]

    chain = [(i, next_on_chain(i)) for i in range(owners)]
    upward = lambda i: (i // 2 + i) % 2 == 0
    onward = to_next_section(lambda i: i if upward(i) else next_on_chain(i))
    first_section = lax.axis_index("sec") == 0

    swap = lambda value: lax.ppermute(value, "own", partner)
    pass_on = lambda value: lax.ppermute(value, "own", chain)
    leave = lambda value: lax.ppermute(value, ("sec", "own"), onward)

    ticks, width, _ = right_sides.shape
    rows = width // STREAMS
    streams = range(STREAMS)
    solved_all = []
    for tick in range(ticks):
        if tick == 0:
            fixed, solved, lhs, gives, keeps = first_step(
                chips,
                STREAMS,
                rows,
                (ancestor, structure, right_sides, carried, inv_diag, factor_tiles),
            )
        else:
            solved, lhs, gives, keeps = next_step(
                chips, tick, fixed, right_sides, moving, crossed
            )
        solved_all.append(solved)
        later_gives, later_keeps = late_step(chips, STREAMS, fixed, lhs)
        moving = []
        for stream in streams:
            taken = swap(gives[stream])
            later = swap(later_gives[stream])
            value = keeps[stream] + taken
            for step in range(chips // 2 - 1):
                value = pass_on(value)
                part = slice(2 * step, 2 * step + 2)
                value = later_keeps[stream][part] + later[part] + value
            value = leave(value)
            moving.append(value)
        crossed = swap(jnp.concatenate([value[1] for value in moving], axis=0))
    carry = jnp.concatenate([value[0] for value in moving], axis=0) + crossed
    carry = jnp.where(first_section, 0.0, carry)
    return jnp.stack(solved_all), carry


def solution(mesh):
    in_specs = (
        P(None, None, ("sec", "own")),
        P(("sec", "own"), None),
        P(("sec", "own"), None),
        P(("sec", "own"), None),
        P("sec", None),
        P(None, ("sec", "own")),
    )
    out_specs = (P(None, None, ("sec", "own")), P(None, ("sec", "own")))
    return jax.shard_map(
        shards,
        mesh=mesh,
        in_specs=in_specs,
        out_specs=out_specs,
        check_vma=False,
    )
```

```python
import functools

import jax
import jax.numpy as jnp
from jax import lax
from jax.experimental import pallas as pl
from jax.experimental.pallas import tpu as pltpu
from jax.sharding import PartitionSpec as P


STREAMS = 4


def split(value):
    high = value.astype(jnp.bfloat16)
    return high, (value - high.astype(jnp.float32)).astype(jnp.bfloat16)


def dot(a, b):
    return jnp.dot(a, b, preferred_element_type=jnp.float32)


def product(table, lhs, factor, place, distance, to_core):
    chips, chip = place
    rows, block = lhs.shape[0] // 2, lhs.shape[1]
    target = ((chip + distance + chips) % chips) * 2 + to_core
    start = pl.multiple_of(table[0, target] * block, block)
    both = dot(lhs, factor[:, pl.ds(start, block)])
    return (both[:rows] + both[rows:]) * table[1, target].astype(jnp.float32)


def position(chips):
    me = lax.axis_index("own")
    chip, core = me // 2, me % 2
    return (chips, chip), core, 1 - 2 * ((chip + core) % 2)


def solve(residual, inverse_high, inverse_low):
    rows = residual.shape[0]
    high, low = split(residual)
    both = dot(jnp.concatenate([high, low], axis=0), inverse_high)
    result = both[:rows] + both[rows:] + dot(high, inverse_low)
    return result, jnp.concatenate(split(result), axis=0)


def parts_of_step(chips, step):
    _, core, ahead = position(chips)
    last = chips // 2 - 1 - step
    up, down = last, -last - 1
    mine = jnp.where(ahead == 1, up, down)
    other = up + down - mine
    for give, distance, first in (
        (True, other, (core + 1 + other) % 2),
        (False, mine, (core + mine) % 2),
    ):
        yield give, 0, distance, (first + 2) % 2
        yield give, 1, distance, (3 - first) % 2


def put_step(table, lhs, factor, chips, step, give, keep, offset):
    rows = keep[0].shape[1]
    place = position(chips)[0]
    for given, index, distance, to_core in parts_of_step(chips, step):
        whole = product(table, lhs, factor, place, distance, to_core)
        for stream, ref in enumerate(give if given else keep):
            ref[offset + index] = whole[stream * rows : (stream + 1) * rows]


def first_kernel(
    chips, streams, ancestor, structure, right_sides, carried, inverse, factor,
    table, factor_here, inverse_high, inverse_low, solved, lhs, *rest,
):
    early, keep = rest[:streams], rest[streams : 2 * streams]
    slots, present, right_here, carried_here, inverse_here, sems = rest[2 * streams :]
    copies = [
        pltpu.make_async_copy(source, target, sems.at[i])
        for i, (source, target) in enumerate(
            (
                (inverse, inverse_here),
                (right_sides.at[0], right_here),
                (carried, carried_here),
                (ancestor, slots),
                (structure, present),
                (factor, factor_here),
            )
        )
    ]
    for copy in copies:
        copy.start()
    for copy in copies[:3]:
        copy.wait()
    inverse_high[...], inverse_low[...] = split(inverse_here[...])
    solved[...], lhs[...] = solve(
        right_here[...] - carried_here[...], inverse_high[...], inverse_low[...]
    )
    copies[3].wait()
    copies[4].wait()
    for slot in range(slots.shape[1]):
        table[0, slots[0, slot]] = slot
        table[1, slots[0, slot]] = present[0, slot]
    copies[5].wait()
    put_step(table, lhs[...], factor_here, chips, 0, early, keep, 0)


def next_kernel(
    chips, streams, tick, table, right_sides, crossed,
    inverse_high, inverse_low, factor, *rest,
):
    moving, (solved, lhs), outs = rest[:streams], rest[streams : streams + 2], rest[streams + 2 :]
    incoming = jnp.concatenate([part[0] for part in moving], axis=0) + crossed[...]
    incoming = jnp.where(lax.axis_index("sec") == 0, 0.0, incoming)
    solved[...], lhs[...] = solve(
        right_sides[tick] - incoming, inverse_high[...], inverse_low[...]
    )
    put_step(table, lhs[...], factor, chips, 0, outs[:streams], outs[streams:], 0)


def late_kernel(chips, streams, table, factor, lhs, *outs):
    value = lhs[...]
    for step in range(1, chips // 2):
        put_step(
            table, value, factor, chips, step,
            outs[:streams], outs[streams:], 2 * (step - 1),
        )


VMEM = pl.BlockSpec(memory_space=pltpu.VMEM)
SMEM = pl.BlockSpec(memory_space=pltpu.SMEM)
HBM = pl.BlockSpec(memory_space=pltpu.HBM)
F32 = functools.partial(jax.ShapeDtypeStruct, dtype=jnp.float32)
BF16 = functools.partial(jax.ShapeDtypeStruct, dtype=jnp.bfloat16)


def call(kernel, products, in_specs, outs, limit, scratch=()):
    return pl.pallas_call(
        kernel,
        out_shape=outs,
        in_specs=in_specs,
        out_specs=[SMEM if out.dtype == jnp.int32 else VMEM for out in outs],
        scratch_shapes=list(scratch),
        compiler_params=pltpu.CompilerParams(vmem_limit_bytes=limit << 20),
        cost_estimate=pl.CostEstimate(
            flops=products * 2 * 256 * 256 * 256,
            bytes_accessed=products * 65536 * 2,
            transcendentals=0,
        ),
    )


def first_step(chips, streams, rows, arrays):
    ancestor, _, _, carried, _, factor = arrays
    slots = ancestor.shape[1]
    width, block = carried.shape
    square = (block, block)
    outs = [jax.ShapeDtypeStruct((2, slots), jnp.int32), BF16(factor.shape)]
    outs += [BF16(square)] * 2 + [F32((width, block)), BF16((2 * width, block))]
    outs += [F32((2, rows, block))] * (2 * streams)
    scratch = [
        pltpu.SMEM((1, slots), jnp.int32),
        pltpu.SMEM((1, slots), jnp.int32),
        pltpu.VMEM((width, block), jnp.float32),
        pltpu.VMEM((width, block), jnp.float32),
        pltpu.VMEM(square, jnp.float32),
        pltpu.SemaphoreType.DMA((6,)),
    ]
    kernel = functools.partial(first_kernel, chips, streams)
    out = call(kernel, 6, [HBM] * 6, outs, 4, scratch)(
        *[pltpu.with_memory_space_constraint(array, pltpu.HBM) for array in arrays]
    )
    fixed, (solved, lhs) = out[:4], out[4:6]
    return fixed, solved, lhs, out[6 : 6 + streams], out[6 + streams :]


def next_step(chips, tick, fixed, right_sides, moving, crossed):
    table, factor, inverse_high, inverse_low = fixed
    streams = len(moving)
    _, rows, block = moving[0].shape
    outs = [F32(crossed.shape), BF16((2 * streams * rows, block))]
    outs += [F32((2, rows, block))] * (2 * streams)
    kernel = functools.partial(next_kernel, chips, streams, tick)
    out = call(kernel, 6, [SMEM] + [VMEM] * (5 + streams), outs, 4)(
        table, right_sides, crossed, inverse_high, inverse_low, factor, *moving
    )
    return out[0], out[1], out[2 : 2 + streams], out[2 + streams :]


def late_step(chips, streams, fixed, lhs):
    rows, block = lhs.shape[0] // 2 // streams, lhs.shape[1]
    outs = [F32((chips - 2, rows, block))] * (2 * streams)
    kernel = functools.partial(late_kernel, chips, streams)
    out = call(kernel, 16, [SMEM, VMEM, VMEM], outs, 4)(fixed[0], fixed[1], lhs)
    return out[:streams], out[streams:]


def shards(right_sides, inv_diag, factor_tiles, structure, ancestor, carried):
    owners = lax.axis_size("own")
    sections = lax.axis_size("sec")
    chips = owners // 2
    partner = [(i, i ^ 1) for i in range(owners)]

    def next_on_chain(i):
        chip, core = i // 2, i % 2
        ahead = 1 - 2 * ((chip + core) % 2)
        return ((chip + ahead) % chips) * 2 + 1 - core

    def to_next_section(place):
        return [
            (s * owners + i, (s + 1) % sections * owners + place(i))
            for s in range(sections)
            for i in range(owners)
        ]

    chain = [(i, next_on_chain(i)) for i in range(owners)]
    upward = lambda i: (i // 2 + i) % 2 == 0
    onward = to_next_section(lambda i: i if upward(i) else next_on_chain(i))
    first_section = lax.axis_index("sec") == 0

    swap = lambda value: lax.ppermute(value, "own", partner)
    pass_on = lambda value: lax.ppermute(value, "own", chain)
    leave = lambda value: lax.ppermute(value, ("sec", "own"), onward)

    ticks, width, _ = right_sides.shape
    rows = width // STREAMS
    streams = range(STREAMS)
    solved_all = []
    for tick in range(ticks):
        if tick == 0:
            fixed, solved, lhs, gives, keeps = first_step(
                chips,
                STREAMS,
                rows,
                (ancestor, structure, right_sides, carried, inv_diag, factor_tiles),
            )
        else:
            solved, lhs, gives, keeps = next_step(
                chips, tick, fixed, right_sides, moving, crossed
            )
        solved_all.append(solved)
        later_gives, later_keeps = late_step(chips, STREAMS, fixed, lhs)
        moving = []
        for stream in streams:
            taken = swap(gives[stream])
            later = swap(later_gives[stream])
            value = keeps[stream] + taken
            for step in range(chips // 2 - 1):
                value = pass_on(value)
                part = slice(2 * step, 2 * step + 2)
                value = later_keeps[stream][part] + later[part] + value
            value = leave(value)
            moving.append(value)
        crossed = swap(jnp.concatenate([value[1] for value in moving], axis=0))
    carry = jnp.concatenate([value[0] for value in moving], axis=0) + crossed
    carry = jnp.where(first_section, 0.0, carry)
    return jnp.stack(solved_all), carry


def solution(mesh):
    in_specs = (
        P(None, None, ("sec", "own")),
        P(("sec", "own"), None),
        P(("sec", "own"), None),
        P(("sec", "own"), None),
        P("sec", None),
        P(None, ("sec", "own")),
    )
    out_specs = (P(None, None, ("sec", "own")), P(None, ("sec", "own")))
    return jax.shard_map(
        shards,
        mesh=mesh,
        in_specs=in_specs,
        out_specs=out_specs,
        check_vma=False,
    )
```
